32 devices in a mesh: dp: 4 (over x, core), vocab: 8 (over z, y).
Axes of the slice: x: 2, y: 2, z: 4, core: 2. Of those that a mesh axis runs over, the one named last changes fastest.
Arguments:
- enc_ids: int32 [64, 256], P('dp'), may hold values from 0 to 32127
- dec_ids: int32 [64, 128], P('dp'), may hold values from 0 to 32127
- dec_mask: int32 [64, 128], P('dp'), may hold values from 0 to 1, as said below
- s_attn: float32 [12, 512, 512], P(None, ('dp', 'vocab'))
- s_ffn: float32 [2, 512, 4096], P(None, ('dp', 'vocab')), may hold values from -0.25 to 0.25
- s_gains: float32 [7, 512], P(None, ('dp', 'vocab')), may hold values from 0.5 to 1.5
- s_table: float32 [32128, 512], P(('vocab', 'dp')), may hold values from -12 to 12
- s_attn_m: float32 [12, 512, 512], P(None, ('dp', 'vocab')), may hold values from -1.9073486e-06 to 1.9073486e-06
- s_attn_v: float32 [12, 512, 512], P(None, ('dp', 'vocab')), may hold values from 1e-14 to 1e-12
- s_ffn_m: float32 [2, 512, 4096], P(None, ('dp', 'vocab')), may hold values from -1.9073486e-06 to 1.9073486e-06
- s_ffn_v: float32 [2, 512, 4096], P(None, ('dp', 'vocab')), may hold values from 1e-14 to 1e-12
- s_gains_m: float32 [7, 512], P(None, ('dp', 'vocab')), may hold values from -1.9073486e-06 to 1.9073486e-06
- s_gains_v: float32 [7, 512], P(None, ('dp', 'vocab')), may hold values from 1e-14 to 1e-12
- s_table_m: float32 [32128, 512], P(('vocab', 'dp')), may hold values from -3.7252903e-08 to 3.7252903e-08
- s_table_v: float32 [32128, 512], P(('vocab', 'dp')), may hold values from 3e-18 to 3e-15
- t_attn: bfloat16 [12, 1024, 1024], P(None, ('dp', 'vocab'))
- t_ffn: bfloat16 [2, 1024, 8448], P(None, ('dp', 'vocab')), may hold values from -0.1875 to 0.1875
- t_gains: bfloat16 [7, 1024], P(None, ('dp', 'vocab')), may hold values from 0.5 to 1.5
- t_embed: bfloat16 [32128, 1024], P('vocab', 'dp'), may hold values from -6 to 6
- t_head: bfloat16 [32128, 1024], P('vocab', 'dp'), may hold values from -0.375 to 0.375
Outputs:
- attn_m_new: float32 [12, 512, 512], P(None, ('dp', 'vocab'))
- attn_v_new: float32 [12, 512, 512], P(None, ('dp', 'vocab'))
- attn_update: float32 [12, 512, 512], P(None, ('dp', 'vocab'))
- ffn_m_new: float32 [2, 512, 4096], P(None, ('dp', 'vocab'))
- ffn_v_new: float32 [2, 512, 4096], P(None, ('dp', 'vocab'))
- ffn_update: float32 [2, 512, 4096], P(None, ('dp', 'vocab'))
- gains_m_new: float32 [7, 512], P(None, ('dp', 'vocab'))
- gains_v_new: float32 [7, 512], P(None, ('dp', 'vocab'))
- gains_update: float32 [7, 512], P(None, ('dp', 'vocab'))
- table_m_new: float32 [32128, 512], P(('vocab', 'dp'))
- table_v_new: float32 [32128, 512], P(('vocab', 'dp'))
- table_update: float32 [32128, 512], P(('vocab', 'dp'))
- tensor_norm: float32 [2, 24], replicated
- grad_norm: float32 [], replicated
- loss: float32 [], replicated
The draws below stay inside these ranges and needn't reach their ends.
Inputs may be any that keep to these rules, and one draw needn't show every extreme that they name: `dec_mask`: each row is 1 on its first L positions and 0 after them, with L from 8 to 128; the first row has L = 128 and the second L = 8.
All inputs are finite; a program needn't handle non-finite values.
Results may differ from the reference program's by a relative error of at most 0.0095.
Values may be sent and summed in bfloat16 or wider, within the bound.
No kernel may reach another device: no remote copies, remote signals or barrier semaphores. Data moves between devices by JAX's collectives and lax.ppermute only.
A program may use at most 384 MiB of HBM per device.

```python
import math
import jax
import jax.numpy as jnp
import numpy as np
from jax import lax

D_S = 512
FF_S = 2048
D_T = 1024
FF_T = 2816
HDIM = 64
V = 32128
ENC_LEN = 256
DEC_LEN = 128
LEN_MIN = 8
SEQ_DEV = 1
BATCH = 64
N_VOCAB = 8


def attn_stack(key, width):
    base = jax.random.normal(key, (12, width, width), jnp.float32) * width ** (-0.5)
    factor = jnp.where(jnp.arange(12) % 4 == 3, 4.0, 1.0)
    return base * factor[:, None, None]


def draw_s_attn(key, part):
    return attn_stack(jax.random.fold_in(key, 11), D_S)


def draw_t_attn(key, part):
    return attn_stack(jax.random.fold_in(key, 23), D_T).astype(jnp.bfloat16)


def draw_dec_mask(key, part):
    lengths = jax.random.randint(jax.random.fold_in(key, 37), (BATCH,), LEN_MIN, DEC_LEN + 1)
    lengths = lengths.at[0].set(DEC_LEN).at[1].set(LEN_MIN)
    position = jnp.arange(DEC_LEN, dtype=jnp.int32)
    return (position[None, :] < lengths[:, None]).astype(jnp.int32)


def touch_ends(result, own_key, least, top_value):
    spot = [jax.random.randint(jax.random.fold_in(own_key, axis), (), 0, length) for axis, length in enumerate(result.shape)]
    longest = result.shape.index(max(result.shape))
    neighbour = spot[:longest] + [(spot[longest] + 1) % result.shape[longest]] + spot[longest + 1:]
    return result.at[tuple(spot)].set(least).at[tuple(neighbour)].set(top_value)


def level_of(rng, extent, shards, low, largest):
    def one(dim, shards_of):
        draws = jax.random.uniform(jax.random.fold_in(jax.random.fold_in(rng, 6), dim), (shards_of,), jnp.float32, low / len(shards), largest / len(shards))
        return jnp.repeat(jnp.exp(draws), extent[dim] // shards_of).reshape((-1,) + (1,) * (len(extent) - dim - 1))

    loudness = one(*shards[0])
    for cut in shards[1:]:
        loudness = loudness * one(*cut)
    return loudness


def cumulative_ranks(count, lean):
    weights = [(1 << 20) // math.isqrt(rank ** lean) + 1 for rank in range(1, count + 1)]
    scale = 1 + sum(weights) // (1 << 30)
    return np.cumsum(np.array([max(1, weight // scale) for weight in weights]))


def ranked(rng, shape, amount, skew):
    table = cumulative_ranks(amount, skew)
    lot = jax.random.randint(jax.random.fold_in(rng, 1), shape, 0, int(table[amount - 1]))
    rank = jnp.searchsorted(jnp.asarray(table, jnp.int32), lot, side="right")
    return jax.random.permutation(jax.random.fold_in(rng, 2), amount)[rank].astype(jnp.int32)


def centred(key, dims, scale, limit, cuts=(), kind=jnp.bfloat16):
    entries = jax.random.normal(key, dims, jnp.float32) * scale
    if len(cuts) > 0:
        entries = level_of(key, dims, cuts, -0.22, 0.18) * entries
    return jnp.clip(entries, min=-limit, max=limit).astype(kind)


def setup_inputs(seed: int = 0) -> dict:
    splits = jax.random.split(jax.random.key(seed), 21)
    return {
        "enc_ids": touch_ends(ranked(splits[0], (BATCH, ENC_LEN), V, 2), jax.random.fold_in(splits[0], 3), 0, V - 1).astype(jnp.int32),
        "dec_ids": touch_ends(ranked(splits[1], (BATCH, DEC_LEN), V, 2), jax.random.fold_in(splits[1], 3), 0, V - 1).astype(jnp.int32),
        "dec_mask": draw_dec_mask(jax.random.fold_in(splits[20], 71), 0),
        "s_attn": draw_s_attn(jax.random.fold_in(splits[20], 71), 0),
        "s_ffn": centred(splits[4], (2, D_S, 2 * FF_S), D_S ** -0.5, 0.25, ((1, 32),), jnp.float32),
        "s_gains": jnp.clip(1.0 + 0.1 * jax.random.normal(splits[5], (7, D_S), jnp.float32), 0.5, 1.5),
        "s_table": centred(splits[6], (V, D_S), 2.0, 12.0, ((0, 32),), jnp.float32),
        "s_attn_m": centred(splits[7], (12, D_S, D_S), (3e-7), 1.9073486328125e-06, ((1, 32),), jnp.float32),
        "s_attn_v": jnp.clip(jnp.exp(math.log(9.999999960041972e-13) - 4.6051702 * jax.random.uniform(splits[8], (12, D_S, D_S), jnp.float32) ** level_of(splits[8], (12, D_S, D_S), ((1, 32),), -0.2, 0.2)), 9.9999998245167e-15, 9.999999960041972e-13),
        "s_ffn_m": centred(splits[9], (2, D_S, 2 * FF_S), (3e-7), 1.9073486328125e-06, ((1, 32),), jnp.float32),
        "s_ffn_v": jnp.clip(jnp.exp(math.log(9.999999960041972e-13) - 4.6051702 * jax.random.uniform(splits[10], (2, D_S, 2 * FF_S), jnp.float32) ** level_of(splits[10], (2, D_S, 2 * FF_S), ((1, 32),), -0.2, 0.2)), 9.9999998245167e-15, 9.999999960041972e-13),
        "s_gains_m": centred(splits[11], (7, D_S), (3e-7), 1.9073486328125e-06, ((1, 32),), jnp.float32),
        "s_gains_v": jnp.clip(jnp.exp(math.log(9.999999960041972e-13) - 4.6051702 * jax.random.uniform(splits[12], (7, D_S), jnp.float32) ** level_of(splits[12], (7, D_S), ((1, 32),), -0.2, 0.2)), 9.9999998245167e-15, 9.999999960041972e-13),
        "s_table_m": centred(splits[13], (V, D_S), (6e-9), 3.725290298461914e-08, ((0, 32),), jnp.float32),
        "s_table_v": jnp.clip(jnp.exp(math.log(2.9999999050033628e-15) - 6.9077552 * jax.random.uniform(splits[14], (V, D_S), jnp.float32) ** level_of(splits[14], (V, D_S), ((0, 32),), -0.2, 0.2)), 3.0000000340435383e-18, 2.9999999050033628e-15),
        "t_attn": draw_t_attn(jax.random.fold_in(splits[20], 71), 0),
        "t_ffn": centred(splits[16], (2, D_T, 3 * FF_T), D_T ** -0.5, 0.1875, ((1, 32),)),
        "t_gains": jnp.clip(1.0 + 0.1 * jax.random.normal(splits[17], (7, D_T), jnp.float32), 0.5, 1.5).astype(jnp.bfloat16),
        "t_embed": centred(splits[18], (V, D_T), 1.0, 6.0, ((0, 8), (1, 4))),
        "t_head": centred(splits[19], (V, D_T), (2 * D_T ** -0.5), 0.375, ((0, 8), (1, 4))),
    }


highest = lax.Precision.HIGHEST
masked_score = -1000000000.0
beta_one = 0.9
beta_two = 0.99
adam_eps = 1e-10
decay = 0.01
rate = 0.05
clip_at = 0.003
step_count = 10

@jax.custom_vjp
def low(v):
    return lax.optimization_barrier(v.astype(jnp.bfloat16)).astype(jnp.float32)

@jax.custom_vjp
def low_back(v):
    return v

def low_keep(v):
    return (low(v), None)

def low_pass(kept, grad):
    return (grad,)

def back_keep(v):
    return (v, None)

def back_low(kept, grad):
    return (low(grad),)
low.defvjp(low_keep, low_pass)
low_back.defvjp(back_keep, back_low)

def low_both(value):
    return low(low_back(value))

def matmul(left_operand, right_operand):
    return jnp.matmul(left_operand, right_operand, precision=highest)

def rms(residual_stream, gain_row):
    return residual_stream * lax.rsqrt(lax.optimization_barrier(jnp.mean(residual_stream * residual_stream, axis=-1, keepdims=True)) + 1e-06) * gain_row

def attend(normed, memory, weights, causal):
    batch_size, length_total, width = normed.shape
    heads = width // HDIM
    query = low_both(matmul(normed, weights[0])).reshape(batch_size, length_total, heads, HDIM)
    key_val = low_both(matmul(memory, weights[1])).reshape(batch_size, memory.shape[1], heads, HDIM)
    value = low_both(matmul(memory, weights[2])).reshape(batch_size, memory.shape[1], heads, HDIM)
    scores = jnp.einsum('bqhd,bkhd->bhqk', query, key_val, precision=highest) * HDIM ** (-0.5)
    if causal:
        rows_idx = lax.broadcasted_iota(jnp.int32, scores.shape, 2)
        cols_idx = lax.broadcasted_iota(jnp.int32, scores.shape, 3)
        scores = jnp.where(cols_idx <= rows_idx, scores, masked_score)
    scores = low_back(scores)
    attn_prob = low(jax.nn.softmax(scores, axis=-1))
    context = jnp.einsum('bhqk,bkhd->bqhd', attn_prob, value, precision=highest)
    context = low_both(context.reshape(batch_size, length_total, width))
    return low_back(matmul(context, weights[3]))

def relu_ffn(normed, weight_matrix):
    halfway = weight_matrix.shape[1] // 2
    pre_act = low_back(matmul(normed, weight_matrix[:, :halfway]))
    hidden = low(jnp.maximum(pre_act, 0.0))
    return low_back(jnp.einsum('blf,df->bld', hidden, weight_matrix[:, halfway:], precision=highest))

def gated_ffn(normed, weight_matrix):
    columns = weight_matrix.shape[1] // 3
    gate_in = matmul(normed, weight_matrix[:, :columns])
    up_in = matmul(normed, weight_matrix[:, columns:2 * columns])
    hidden = low(jax.nn.gelu(gate_in, approximate=True) * up_in)
    return jnp.einsum('blf,df->bld', hidden, weight_matrix[:, 2 * columns:], precision=highest)

def encoder(residual_stream, attn, ffn, gains, ffn_fn):
    normed = low(rms(residual_stream, gains[0]))
    residual_stream = residual_stream + attend(normed, normed, attn[0:4], False)
    residual_stream = residual_stream + ffn_fn(low(rms(residual_stream, gains[1])), ffn[0])
    return low(rms(residual_stream, gains[2]))

def decoder(residual_stream, memory, attn, ffn, gains, ffn_fn, out_scale):
    normed = low(rms(residual_stream, gains[3]))
    residual_stream = residual_stream + attend(normed, normed, attn[4:8], True)
    residual_stream = residual_stream + attend(low(rms(residual_stream, gains[4])), memory, attn[8:12], False)
    residual_stream = residual_stream + ffn_fn(low(rms(residual_stream, gains[5])), ffn[1])
    return low(rms(residual_stream, gains[6]) * out_scale)

def block_loss(params, teacher, block_data):
    attn, ffn, gains, table = params
    t_attn, t_ffn, t_gains, t_embed, t_head = teacher
    enc_block, dec_block, row_weight = block_data
    memory = encoder(table[enc_block], attn, ffn, gains, relu_ffn)
    student_in = decoder(table[dec_block], memory, attn, ffn, gains, relu_ffn, D_S ** (-0.5))
    student_logit = low_back(jnp.einsum('bld,vd->blv', student_in, table, precision=highest))
    t_memory = encoder(t_embed[enc_block], t_attn, t_ffn, t_gains, gated_ffn)
    teacher_in = decoder(t_embed[dec_block], t_memory, t_attn, t_ffn, t_gains, gated_ffn, 1.0)
    teacher_logit = jnp.einsum('bld,vd->blv', teacher_in, t_head, precision=highest)
    student_log = jax.nn.log_softmax(student_logit, axis=-1)
    teacher_log = jax.nn.log_softmax(teacher_logit, axis=-1)
    kl_row = lax.optimization_barrier(jnp.sum(jnp.exp(teacher_log) * (teacher_log - student_log), axis=-1))
    return jnp.sum(row_weight * kl_row)

def moments(grad_part, first_part, second_part, master):
    new_first = beta_one * first_part + (1.0 - beta_one) * grad_part
    new_second = beta_two * second_part + (1.0 - beta_two) * grad_part * grad_part
    direction = new_first / (1.0 - beta_one ** step_count) / (jnp.sqrt(new_second / (1.0 - beta_two ** step_count)) + adam_eps) + decay * master
    return (new_first, new_second, direction)

def tensor_sums(arrays):
    attn, ffn, gains, table = arrays
    halfway = ffn.shape[2] // 2
    ffn_parts = jnp.stack([lax.optimization_barrier(jnp.sum(ffn[:, :, :halfway] ** 2, axis=(1, 2))), lax.optimization_barrier(jnp.sum(ffn[:, :, halfway:] ** 2, axis=(1, 2)))], axis=1).reshape(-1)
    return jnp.concatenate([lax.optimization_barrier(jnp.sum(attn * attn, axis=(1, 2))), ffn_parts, lax.optimization_barrier(jnp.sum(gains * gains, axis=1)), jnp.sum(table * table).reshape(1)])

def expand_ratios(ratio, halfway):
    ffn_ratio = jnp.repeat(ratio[12:16].reshape(2, 2), halfway, axis=1)[:, None, :]
    return (ratio[:12][:, None, None], ffn_ratio, ratio[16:23][:, None], ratio[23])

def reference(enc_ids, dec_ids, dec_mask, s_attn, s_ffn, s_gains, s_table, s_attn_m, s_attn_v, s_ffn_m, s_ffn_v, s_gains_m, s_gains_v, s_table_m, s_table_v, t_attn, t_ffn, t_gains, t_embed, t_head):
    teacher = tuple((arr.astype(jnp.float32) for arr in (t_attn, t_ffn, t_gains, t_embed, t_head)))
    end_mask = dec_mask.astype(jnp.float32)
    row_weight = end_mask / (lax.optimization_barrier(jnp.sum(end_mask, axis=1, keepdims=True)) * BATCH)
    block_size = SEQ_DEV * N_VOCAB
    block_count = BATCH // block_size
    blocks = (enc_ids.reshape(block_count, block_size, ENC_LEN), dec_ids.reshape(block_count, block_size, DEC_LEN), row_weight.reshape(block_count, block_size, DEC_LEN))
    masters = (s_attn, s_ffn, s_gains, s_table)

    def total_loss(params):
        low_params = tuple((low(part) for part in params))

        def step(running, block_data):
            return (running + jax.checkpoint(block_loss)(low_params, teacher, block_data), None)
        total, _ = lax.scan(step, jnp.zeros((), jnp.float32), blocks)
        return total
    loss, pull = jax.vjp(total_loss, masters)
    gradients, = pull(jnp.ones((), jnp.float32))
    square_sum = sum((jnp.sum(part * part) for part in gradients))
    grad_norm = jnp.sqrt(square_sum)
    factor = jnp.minimum(1.0, clip_at / grad_norm)
    firsts = (s_attn_m, s_ffn_m, s_gains_m, s_table_m)
    seconds = (s_attn_v, s_ffn_v, s_gains_v, s_table_v)
    states = [moments(grad_part * factor, first_part, second_part, master) for grad_part, first_part, second_part, master in zip(gradients, firsts, seconds, masters)]
    directions = tuple((state[2] for state in states))
    tensor_norm = jnp.sqrt(jnp.stack([tensor_sums(masters), tensor_sums(directions)]))
    ratio = tensor_norm[0] / (tensor_norm[1] + 1e-06)
    expanded = expand_ratios(ratio, s_ffn.shape[2] // 2)
    updates = [-rate * scale_part * state[2] for scale_part, state in zip(expanded, states)]
    return (states[0][0], states[0][1], updates[0], states[1][0], states[1][1], updates[1], states[2][0], states[2][1], updates[2], states[3][0], states[3][1], updates[3], tensor_norm, grad_norm, loss)
```

```python
import jax
import jax.numpy as jnp
from jax import lax
from jax.sharding import PartitionSpec as P

D_S = 512
HDIM = 64
LANES = 128


masked_score = -1000000000.0
beta_one = 0.9
beta_two = 0.99
adam_eps = 1e-10
decay = 0.01
rate = 0.05
clip_at = 0.003
step_count = 10

BF = jnp.bfloat16
F32 = jnp.float32


def swap(value, axis, flip):
    count = lax.axis_size(axis)
    return lax.ppermute(value, axis, [(i, i ^ flip) for i in range(count)])


def trade(blocks, axis):
    return [blocks[0]] + [swap(blocks[k], axis, k) for k in range(1, len(blocks))]


def spread(value, axis):
    return trade([value] * lax.axis_size(axis), axis)


def relative(value, axis, dim=0):
    order = jnp.arange(lax.axis_size(axis)) ^ lax.axis_index(axis)
    return jnp.take(value, order, axis=dim)


def flips(axis):
    count = lax.axis_size(axis)
    bits = count.bit_length() - 1
    return [1 << (bits - 1 - i) for i in range(bits)]


def sum_everywhere(value):
    for axis in ("dp", "vocab"):
        for flip in flips(axis)[::-1]:
            value = value + swap(value, axis, flip)
    return value


def gather_pairs(value, axis):
    parts = {0: value}
    for flip in flips(axis):
        parts.update({k ^ flip: swap(part, axis, flip) for k, part in list(parts.items())})
    index = lax.axis_index(axis)
    out = jnp.zeros((lax.axis_size(axis),) + value.shape, value.dtype)
    for k, part in parts.items():
        out = lax.dynamic_update_index_in_dim(out, part, index ^ k, 0)
    return out


def half_step(value, dim, axis, flip):
    bit = (lax.axis_index(axis) // flip) % 2
    keep = lax.dynamic_index_in_dim(value, bit, dim, keepdims=True)
    sent = lax.dynamic_index_in_dim(value, 1 - bit, dim, keepdims=True)
    return keep.astype(F32) + swap(sent.astype(BF), axis, flip).astype(F32)


def reduce_rows(grad):
    names = [("dp", flip) for flip in flips("dp")] + [("vocab", flip) for flip in flips("vocab")]
    shares = 1 << len(names)
    rows, columns = grad.shape
    grad = grad.reshape((2,) * len(names) + (rows // shares, columns))
    core = len(flips("dp")) - 1
    steps = [i for i in range(len(names)) if i != core]
    last = len(names) - 1
    orders = (steps, [last] + [i for i in steps if i != last])
    grad = half_step(grad, core, *names[core]).astype(BF)
    half = max(LANES, columns // 2 // LANES * LANES)
    pieces = [grad[..., :half], grad[..., half:]] if half < columns else [grad]
    done = []
    for piece, order in zip(pieces, orders):
        for place, i in enumerate(order):
            piece = half_step(piece, i, *names[i])
            if place + 1 < len(order):
                piece = piece.astype(BF)
        done.append(piece.reshape(rows // shares, -1))
    return jnp.concatenate(done, axis=1) if len(done) > 1 else done[0]


def project(residual_stream, weight_matrix):
    return jnp.dot(residual_stream, weight_matrix, preferred_element_type=F32)


def project_back(residual_stream, weight_matrix):
    return jnp.einsum("vim,tm->vit", residual_stream, weight_matrix, preferred_element_type=F32)


def outer_sum(left_operand, right_operand):
    return jnp.einsum("uwf,uwp->fp", left_operand, right_operand, preferred_element_type=F32).astype(
        BF
    )


def split_heads(residual_stream):
    return residual_stream.reshape(
        residual_stream.shape[0], residual_stream.shape[1], residual_stream.shape[2] // HDIM, HDIM
    )


def norm_forward(residual_stream, gain_row):
    inverse = lax.rsqrt(jnp.mean(residual_stream * residual_stream, axis=-1, keepdims=True) + 1e-06)
    return (residual_stream * inverse * gain_row.astype(F32), inverse)


def norm_backward(upstream, residual_stream, inverse, gain_row):
    weighted = upstream * gain_row.astype(F32)
    gain_grad = jnp.sum(upstream * residual_stream * inverse, axis=(0, 1))
    stream_grad = inverse * weighted - residual_stream * inverse**3 * jnp.mean(
        weighted * residual_stream, axis=-1, keepdims=True
    )
    return (stream_grad, gain_grad)


def scores_of(query_low, key_low, causal):
    scores = jnp.einsum(
        "sqhd,skhd->shqk",
        split_heads(query_low),
        split_heads(key_low),
        preferred_element_type=F32,
    ) * HDIM ** (-0.5)
    if causal:
        rows_idx = lax.broadcasted_iota(jnp.int32, scores.shape, 2)
        cols_idx = lax.broadcasted_iota(jnp.int32, scores.shape, 3)
        scores = jnp.where(cols_idx <= rows_idx, scores, masked_score)
    return scores


def attend_forward(query_in, key_in, weights, causal):
    width = weights.shape[0]
    if key_in is None:
        joint = project(query_in, weights[:, : 3 * width]).astype(BF)
        query_low = joint[..., :width]
        joint = joint[..., width:]
    else:
        query_low = project(query_in, weights[:, :width]).astype(BF)
        joint = project(key_in, weights[:, width : 3 * width]).astype(BF)
    key_low, value_low = joint[..., :width], joint[..., width:]
    scores = scores_of(query_low, key_low, causal)
    row_top = jnp.max(scores, axis=-1, keepdims=True)
    shifted = jnp.exp(scores - row_top)
    row_total = jnp.sum(shifted, axis=-1, keepdims=True)
    attn_prob = (shifted / row_total).astype(BF)
    log_total = row_top + jnp.log(row_total)
    context = jnp.einsum(
        "shqk,skhd->sqhd", attn_prob, split_heads(value_low), preferred_element_type=F32
    )
    context = context.reshape(query_in.shape[0], query_in.shape[1], -1).astype(BF)
    return (
        project(context, weights[:, 3 * width :]),
        (query_low, key_low, value_low, context, log_total),
    )


def attend_backward(output_gradient, query_in, key_in, weights, stored, causal):
    width = weights.shape[0]
    query_low, key_low, value_low, context, log_total = stored
    out_low = output_gradient.astype(BF)
    context_grad = project_back(out_low, weights[:, 3 * width :]).astype(BF)
    attn_prob = jnp.exp(scores_of(query_low, key_low, causal) - log_total)
    prob_grad = jnp.einsum(
        "sqhd,skhd->shqk",
        split_heads(context_grad),
        split_heads(value_low),
        preferred_element_type=F32,
    )
    score_grad = (
        attn_prob * (prob_grad - jnp.sum(attn_prob * prob_grad, axis=-1, keepdims=True))
    ).astype(BF)
    query_grad = (
        (
            jnp.einsum(
                "shqk,skhd->sqhd", score_grad, split_heads(key_low), preferred_element_type=F32
            )
            * HDIM ** (-0.5)
        )
        .reshape(query_low.shape)
        .astype(BF)
    )
    key_grad = (
        (
            jnp.einsum(
                "shqk,sqhd->skhd", score_grad, split_heads(query_low), preferred_element_type=F32
            )
            * HDIM ** (-0.5)
        )
        .reshape(key_low.shape)
        .astype(BF)
    )
    value_grad = (
        jnp.einsum(
            "shqk,sqhd->skhd",
            attn_prob.astype(BF),
            split_heads(context_grad),
            preferred_element_type=F32,
        )
        .reshape(value_low.shape)
        .astype(BF)
    )
    if key_in is None:
        joint = jnp.concatenate([query_grad, key_grad, value_grad], axis=-1)
        weight_grad = [outer_sum(query_in, joint), outer_sum(context, out_low)]
        return (project_back(joint, weights[:, : 3 * width]), None, weight_grad)
    joint = jnp.concatenate([key_grad, value_grad], axis=-1)
    weight_grad = [
        outer_sum(query_in, query_grad),
        outer_sum(key_in, joint),
        outer_sum(context, out_low),
    ]
    return (
        project_back(query_grad, weights[:, :width]),
        project_back(joint, weights[:, width : 3 * width]),
        weight_grad,
    )


def relu_forward(normed, weight_matrix):
    halfway = weight_matrix.shape[1] // 2
    pre_act = project(normed, weight_matrix[:, :halfway])
    hidden = jnp.maximum(pre_act, 0.0).astype(BF)
    return (project_back(hidden, weight_matrix[:, halfway:]), (pre_act > 0.0, hidden))


def relu_backward(output_gradient, normed, weight_matrix, stored):
    positive, hidden = stored
    halfway = weight_matrix.shape[1] // 2
    out_low = output_gradient.astype(BF)
    hidden_grad = project(out_low, weight_matrix[:, halfway:])
    pre_grad = jnp.where(positive, hidden_grad, 0.0).astype(BF)
    weight_grad = [outer_sum(normed, pre_grad), outer_sum(out_low, hidden)]
    return (project_back(pre_grad, weight_matrix[:, :halfway]), weight_grad)


def gated_forward(normed, weight_matrix):
    columns = weight_matrix.shape[1] // 3
    hidden = (
        jax.nn.gelu(project(normed, weight_matrix[:, :columns]), approximate=True)
        * project(normed, weight_matrix[:, columns : 2 * columns])
    ).astype(BF)
    return (project_back(hidden, weight_matrix[:, 2 * columns :]), None)


def encoder_forward(residual_stream, attn, ffn, gains, ffn_forward):
    normed_one, inv_one = norm_forward(residual_stream, gains[0])
    normed_one = normed_one.astype(BF)
    branch, attn_stored = attend_forward(normed_one, None, attn, False)
    stream_one = residual_stream + branch
    normed_two, inv_two = norm_forward(stream_one, gains[1])
    normed_two = normed_two.astype(BF)
    branch, ffn_stored = ffn_forward(normed_two, ffn)
    stream_two = stream_one + branch
    result, inv_out = norm_forward(stream_two, gains[2])
    return (
        result.astype(BF),
        (
            inv_one,
            normed_one,
            attn_stored,
            stream_one,
            inv_two,
            normed_two,
            ffn_stored,
            stream_two,
            inv_out,
        ),
    )


def encoder_backward(output_gradient, residual_stream, stored, attn, ffn, gains):
    (
        inv_one,
        normed_one,
        attn_stored,
        stream_one,
        inv_two,
        normed_two,
        ffn_stored,
        stream_two,
        inv_out,
    ) = stored
    grad_two, gain_two = norm_backward(output_gradient, stream_two, inv_out, gains[2])
    normed_grad, ffn_grad = relu_backward(grad_two, normed_two, ffn, ffn_stored)
    grad_part, gain_one = norm_backward(normed_grad, stream_one, inv_two, gains[1])
    grad_one = grad_two + grad_part
    in_grad, _, attn_grad = attend_backward(grad_one, normed_one, None, attn, attn_stored, False)
    grad_part, gain_zero = norm_backward(in_grad, residual_stream, inv_one, gains[0])
    return (grad_one + grad_part, attn_grad, ffn_grad, [gain_zero, gain_one, gain_two])


def decoder_forward(residual_stream, memory, attn, ffn, gains, ffn_forward, out_scale):
    self_attn, cross_attn = attn
    normed_one, inv_one = norm_forward(residual_stream, gains[3])
    normed_one = normed_one.astype(BF)
    branch, self_stored = attend_forward(normed_one, None, self_attn, True)
    stream_one = residual_stream + branch
    normed_two, inv_two = norm_forward(stream_one, gains[4])
    normed_two = normed_two.astype(BF)
    branch, cross_stored = attend_forward(normed_two, memory, cross_attn, False)
    stream_two = stream_one + branch
    normed_three, inv_three = norm_forward(stream_two, gains[5])
    normed_three = normed_three.astype(BF)
    branch, ffn_stored = ffn_forward(normed_three, ffn)
    stream_three = stream_two + branch
    result, inv_out = norm_forward(stream_three, gains[6])
    stored = (
        inv_one,
        normed_one,
        self_stored,
        stream_one,
        inv_two,
        normed_two,
        cross_stored,
        stream_two,
        inv_three,
        normed_three,
        ffn_stored,
        stream_three,
        inv_out,
    )
    return ((result * out_scale).astype(BF), stored)


def decoder_backward(output_gradient, residual_stream, memory, stored, attn, ffn, gains, out_scale):
    (
        inv_one,
        normed_one,
        self_stored,
        stream_one,
        inv_two,
        normed_two,
        cross_stored,
        stream_two,
        inv_three,
        normed_three,
        ffn_stored,
        stream_three,
        inv_out,
    ) = stored
    self_attn, cross_attn = attn
    grad_three, gain_six = norm_backward(
        output_gradient * out_scale, stream_three, inv_out, gains[6]
    )
    normed_grad, ffn_grad = relu_backward(grad_three, normed_three, ffn, ffn_stored)
    grad_part, gain_five = norm_backward(normed_grad, stream_two, inv_three, gains[5])
    grad_two = grad_three + grad_part
    query_in_grad, memory_grad, cross_grad = attend_backward(
        grad_two, normed_two, memory, cross_attn, cross_stored, False
    )
    grad_part, gain_four = norm_backward(query_in_grad, stream_one, inv_two, gains[4])
    grad_one = grad_two + grad_part
    in_grad, _, self_grad = attend_backward(
        grad_one, normed_one, None, self_attn, self_stored, True
    )
    grad_part, gain_three = norm_backward(in_grad, residual_stream, inv_one, gains[3])
    return (
        grad_one + grad_part,
        memory_grad,
        self_grad,
        cross_grad,
        ffn_grad,
        [gain_three, gain_four, gain_five, gain_six],
    )


class Requests:
    def __init__(self, ids, vocab_rows):
        members, tokens = ids.shape
        index = lax.axis_index("vocab")
        self.room = -(-(tokens * 7) // (members * 6 * 16)) * 16
        place = lax.broadcasted_iota(jnp.int32, (1, tokens, tokens), 2)
        same = ids[:, :, None] == ids[:, None, :]
        first = jnp.min(jnp.where(same, place, tokens), axis=2)
        unique = first == jnp.arange(tokens)[None, :]
        shard = ids // vocab_rows
        mine = unique & (shard == index)
        before = (jnp.arange(tokens)[:, None] < jnp.arange(tokens)[None, :]).astype(BF)
        self.place = jnp.dot(mine.astype(BF), before, preferred_element_type=F32).astype(jnp.int32)
        self.mine = mine
        self.local = ids - index * vocab_rows
        near = (shard[0][:, None] == shard[0][None, :]) & unique[0][None, :]
        near = near & (place[0] < first[0][:, None])
        self.own_place = jnp.sum(near.astype(jnp.int32), axis=1)
        self.own_shard = shard[0] ^ index
        of_shard = shard[:, :, None] == jnp.arange(members)[None, None, :]
        counts = jnp.sum((of_shard & unique[:, :, None]).astype(jnp.int32), axis=1)
        most = jnp.max(counts).reshape(1)
        for flip in flips("dp"):
            most = jnp.maximum(most, swap(most, "dp", flip))
        self.rounds = (most[0] + self.room - 1) // self.room

    def listed(self, turn):
        slot = turn * self.room + jnp.arange(self.room)[None, :, None]
        hit = self.mine[:, None, :] & (self.place[:, None, :] == slot)
        rows = jnp.sum(jnp.where(hit, self.local[:, None, :], 0), axis=2)
        return rows, jnp.any(hit, axis=2)

    def chosen(self, turn):
        spot = self.own_place - turn * self.room
        inside = (spot >= 0) & (spot < self.room)
        spot = jnp.where(inside, self.own_shard * self.room + spot, -1)
        return (spot[:, None] == jnp.arange(self.mine.shape[0] * self.room)[None, :]).astype(BF)


def take_rows(table, rows):
    return jnp.take(table, rows.reshape(-1), axis=0).reshape(rows.shape + (table.shape[1],))


def student_rows_of(requests, turn, table):
    rows, _ = requests.listed(turn)
    found = take_rows(table, rows)
    found = jnp.concatenate(trade([found[k] for k in range(found.shape[0])], "vocab"))
    return jnp.dot(requests.chosen(turn), found, preferred_element_type=F32)


def teacher_rows_of(requests, turn, column_part):
    rows, _ = requests.listed(turn)
    asked = spread(rows, "dp")
    found = [take_rows(column_part, rows) for rows in asked]
    found = jnp.stack(trade(found, "dp"), axis=2)
    found = jnp.concatenate(trade([found[k] for k in range(found.shape[0])], "vocab"))
    found = relative(found, "dp", 1).reshape(found.shape[0], -1)
    return jnp.dot(requests.chosen(turn), found, preferred_element_type=F32)


def table_grad_of(requests, turn, embed_grad, vocab_rows):
    rows, used = requests.listed(turn)
    wanted = jnp.einsum("tr,td->rd", requests.chosen(turn), embed_grad, preferred_element_type=F32)
    wanted = wanted.astype(BF).reshape(rows.shape + (embed_grad.shape[1],))
    got = jnp.concatenate(trade([wanted[k] for k in range(wanted.shape[0])], "vocab"))
    rows = jnp.where(used, rows, -1).reshape(-1)
    spots = (jnp.arange(vocab_rows)[:, None] == rows[None, :]).astype(BF)
    return jnp.dot(spots, got, preferred_element_type=F32)


def all_rounds(requests, start, one_round):
    def more(state):
        return state[0] < requests.rounds

    def again(state):
        return state[0] + 1, state[1] + one_round(state[0])

    return lax.while_loop(more, again, (jnp.int32(1), start))[1]


def moments(grad_part, first_part, second_part, master):
    new_first = beta_one * first_part + (1.0 - beta_one) * grad_part
    new_second = beta_two * second_part + (1.0 - beta_two) * grad_part * grad_part
    direction = (
        new_first
        / (1.0 - beta_one**step_count)
        / (jnp.sqrt(new_second / (1.0 - beta_two**step_count)) + adam_eps)
        + decay * master
    )
    return (new_first, new_second, direction)


def tensor_sums(arrays):
    attn, ffn, gains, table = arrays
    halfway = ffn.shape[2] // 2
    ffn_parts = jnp.stack(
        [
            jnp.sum(ffn[:, :, :halfway] ** 2, axis=(1, 2)),
            jnp.sum(ffn[:, :, halfway:] ** 2, axis=(1, 2)),
        ],
        axis=1,
    ).reshape(-1)
    return jnp.concatenate(
        [
            jnp.sum(attn * attn, axis=(1, 2)),
            ffn_parts,
            jnp.sum(gains * gains, axis=1),
            jnp.sum(table * table).reshape(1),
        ]
    )


def expand_ratios(ratio, halfway):
    ffn_ratio = jnp.repeat(ratio[12:16].reshape(2, 2), halfway, axis=1)[:, None, :]
    return (ratio[:12][:, None, None], ffn_ratio, ratio[16:23][:, None], ratio[23])


def side_by_side(matrices):
    return matrices.transpose(1, 0, 2).reshape(matrices.shape[1], -1)


def gather_rows(pieces):
    return lax.all_gather(jnp.concatenate(pieces, axis=1), ("dp", "vocab"), axis=0, tiled=True)


def gain_columns(gains):
    return jnp.pad(gains.T, ((0, 0), (0, LANES - gains.shape[0])))


def body(
    enc_ids,
    dec_ids,
    dec_mask,
    s_attn,
    s_ffn,
    s_gains,
    s_table,
    s_attn_m,
    s_attn_v,
    s_ffn_m,
    s_ffn_v,
    s_gains_m,
    s_gains_v,
    s_table_m,
    s_table_v,
    t_attn,
    t_ffn,
    t_gains,
    t_embed,
    t_head,
):
    vocab_count = lax.axis_size("vocab")
    dp_count = lax.axis_size("dp")
    vocab_index = lax.axis_index("vocab")
    seqs = enc_ids.shape[0]
    seq_dev = seqs // vocab_count
    enc_len = enc_ids.shape[1]
    dec_len = dec_ids.shape[1]
    total_seqs = seqs * dp_count
    width = s_attn.shape[2]
    t_width = t_attn.shape[2]
    ffn_width = s_ffn.shape[2]
    gain_count = s_gains.shape[0]
    out_scale = D_S ** (-0.5)
    vocab_rows = s_table.shape[0] * dp_count

    student = gather_rows(
        [
            side_by_side(s_attn.astype(BF)),
            side_by_side(s_ffn.astype(BF)),
            gain_columns(s_gains.astype(BF)),
        ]
    )
    teacher_enc = gather_rows([side_by_side(t_attn[:4]), t_ffn[0], gain_columns(t_gains)])
    teacher_dec = gather_rows([side_by_side(t_attn[4:]), t_ffn[1]])
    cut = 12 * width
    attn = [student[:, 4 * i * width : 4 * (i + 1) * width] for i in range(3)]
    ffn = [student[:, cut + i * ffn_width : cut + (i + 1) * ffn_width] for i in range(2)]
    gains = student[:, cut + 2 * ffn_width :].T[:gain_count]
    cut = 4 * t_width
    tattn = [teacher_enc[:, :cut], teacher_dec[:, :cut], teacher_dec[:, cut : 2 * cut]]
    tffn = [teacher_enc[:, cut : cut + t_ffn.shape[2]], teacher_dec[:, 2 * cut :]]
    tgains = teacher_enc[:, cut + t_ffn.shape[2] :].T[:gain_count]

    table = gather_pairs(s_table.astype(BF), "dp").reshape(vocab_rows, width)
    ids = jnp.concatenate(
        [enc_ids.reshape(vocab_count, -1), dec_ids.reshape(vocab_count, -1)], axis=1
    )
    requests = Requests(relative(ids, "vocab"), vocab_rows)

    def student_round(turn):
        return student_rows_of(requests, turn, table)

    def teacher_round(turn):
        return teacher_rows_of(requests, turn, t_embed)

    embedded = all_rounds(requests, student_round(jnp.int32(0)), student_round)
    t_embedded = all_rounds(requests, teacher_round(jnp.int32(0)), teacher_round)
    enc_tokens = seq_dev * enc_len

    def parted(rows):
        return (
            rows[:enc_tokens].reshape(seq_dev, enc_len, -1),
            rows[enc_tokens:].reshape(seq_dev, dec_len, -1),
        )

    enc_in, dec_in = parted(embedded)
    t_enc_in, t_dec_in = parted(t_embedded)

    memory, enc_stored = encoder_forward(enc_in, attn[0], ffn[0], gains, relu_forward)
    head_in, dec_stored = decoder_forward(
        dec_in, memory, attn[1:], ffn[1], gains, relu_forward, out_scale
    )
    head_rows = head_in.reshape(-1, width)
    student_rows = jnp.concatenate(spread(head_rows, "vocab"))
    student_logit = lax.dot_general(
        student_rows, table, (((1,), (1,)), ((), ())), preferred_element_type=F32
    )
    student_top = jnp.max(student_logit, axis=1)
    student_total = jnp.sum(jnp.exp(student_logit - student_top[:, None]), axis=1)

    head_parts = {0: t_head}
    for flip in flips("dp"):
        head_parts.update({k ^ flip: swap(part, "dp", flip) for k, part in list(head_parts.items())})
    thead = jnp.concatenate([head_parts[k] for k in range(dp_count)], axis=1)

    t_memory, _ = encoder_forward(t_enc_in, tattn[0], tffn[0], tgains, gated_forward)
    t_head_in, _ = decoder_forward(
        t_dec_in, t_memory, tattn[1:], tffn[1], tgains, gated_forward, 1.0
    )
    t_head_rows = relative(t_head_in.reshape(-1, dp_count, t_head.shape[1]), "dp", 1)
    t_head_rows = t_head_rows.reshape(-1, t_width)
    teacher_rows = jnp.concatenate(spread(t_head_rows, "vocab"))
    teacher_logit = lax.dot_general(
        teacher_rows, thead, (((1,), (1,)), ((), ())), preferred_element_type=F32
    )
    teacher_top = jnp.max(teacher_logit, axis=1)
    teacher_exp = jnp.exp(teacher_logit - teacher_top[:, None])
    teacher_total = jnp.sum(teacher_exp, axis=1)
    teacher_gap = jnp.sum(teacher_exp * (teacher_logit - student_logit), axis=1)

    sums = jnp.stack([student_top, student_total, teacher_top, teacher_total, teacher_gap])
    own_rows = seq_dev * dec_len
    sums = sums.reshape(5, vocab_count, own_rows)
    sums = jnp.stack(total_rows(sums), axis=0)
    student_lse, teacher_lse, kl_row = combine_sums(sums)
    end_mask = relative(dec_mask.astype(F32).reshape(vocab_count, seq_dev, dec_len), "vocab")
    row_weight = end_mask / (jnp.sum(end_mask, axis=2, keepdims=True) * total_seqs)
    row_weight = row_weight.reshape(-1)
    loss_sum = jnp.sum(row_weight[:own_rows] * kl_row[:own_rows])
    logit_grad = (
        row_weight[:, None]
        * (
            jnp.exp(student_logit - student_lse[:, None])
            - jnp.exp(teacher_logit - teacher_lse[:, None])
        )
    ).astype(BF)
    head_parts = jnp.dot(logit_grad, table, preferred_element_type=F32).astype(BF)
    head_parts = head_parts.reshape(vocab_count, own_rows, width)
    head_parts = trade([head_parts[k] for k in range(vocab_count)], "vocab")
    head_grad = sum(part.astype(F32) for part in head_parts).reshape(head_in.shape)
    table_grad = lax.dot_general(
        logit_grad, student_rows, (((0,), (0,)), ((), ())), preferred_element_type=F32
    )

    dec_in_grad, memory_grad, self_grad, cross_grad, dec_ffn_grad, dec_gains = decoder_backward(
        head_grad, dec_in, memory, dec_stored, attn[1:], ffn[1], gains, out_scale
    )
    enc_in_grad, enc_grad, enc_ffn_grad, enc_gains = encoder_backward(
        memory_grad, enc_in, enc_stored, attn[0], ffn[0], gains
    )
    embed_grad = jnp.concatenate(
        [enc_in_grad.reshape(-1, width), dec_in_grad.reshape(-1, width)]
    ).astype(BF)

    def grad_round(turn):
        return table_grad_of(requests, turn, embed_grad, vocab_rows)

    table_grad = all_rounds(requests, table_grad + grad_round(jnp.int32(0)), grad_round)

    groups = [dec_ffn_grad, cross_grad, self_grad, enc_ffn_grad]
    groups.append(enc_grad + [gain_columns(jnp.stack(enc_gains + dec_gains)).astype(BF)])
    owned = [reduce_rows(jnp.concatenate(group, axis=1)) for group in groups]
    dec_ffn_own, cross_own, self_own, enc_ffn_own, enc_own = owned

    def stacked(matrix):
        return matrix.reshape(matrix.shape[0], -1, width).transpose(1, 0, 2)

    attn_shard = jnp.concatenate(
        [stacked(enc_own[:, : 4 * width]), stacked(self_own), stacked(cross_own)]
    )
    ffn_shard = jnp.stack([enc_ffn_own, dec_ffn_own])
    gains_shard = enc_own[:, 4 * width :].T[:gain_count]
    table_shard = table_grad.astype(BF).reshape((2,) * len(flips("dp")) + s_table.shape)
    for place in range(len(flips("dp")) - 1, -1, -1):
        table_shard = half_step(table_shard, place, "dp", flips("dp")[place])
    table_shard = table_shard.reshape(s_table.shape)

    gradients = (attn_shard, ffn_shard, gains_shard, table_shard)
    masters = (s_attn, s_ffn, s_gains, s_table)
    square_sum = sum((jnp.sum(part * part) for part in gradients))
    totals = jnp.concatenate([jnp.stack([square_sum, loss_sum]), tensor_sums(masters)])
    totals = sum_everywhere(totals)
    grad_norm = jnp.sqrt(totals[0])
    loss = totals[1]
    factor = jnp.minimum(1.0, clip_at / grad_norm)
    firsts = (s_attn_m, s_ffn_m, s_gains_m, s_table_m)
    seconds = (s_attn_v, s_ffn_v, s_gains_v, s_table_v)
    states = [
        moments(grad_part * factor, first_part, second_part, master)
        for grad_part, first_part, second_part, master in zip(gradients, firsts, seconds, masters)
    ]
    directions = tuple((state[2] for state in states))
    tensor_norm = jnp.sqrt(jnp.stack([totals[2:], sum_everywhere(tensor_sums(directions))]))
    ratio = tensor_norm[0] / (tensor_norm[1] + 1e-06)
    expanded = expand_ratios(ratio, s_ffn.shape[2] // 2)
    updates = [-rate * scale_part * state[2] for scale_part, state in zip(expanded, states)]
    return (
        states[0][0],
        states[0][1],
        updates[0],
        states[1][0],
        states[1][1],
        updates[1],
        states[2][0],
        states[2][1],
        updates[2],
        states[3][0],
        states[3][1],
        updates[3],
        tensor_norm,
        grad_norm,
        loss,
    )


def total_rows(sums):
    parts = [sums]
    for k in range(1, lax.axis_size("vocab")):
        other = swap(sums, "vocab", k)
        order = [i ^ k for i in range(sums.shape[1])]
        parts.append(jnp.stack([other[:, i] for i in order], axis=1))
    return parts


def combine_sums(sums):
    student_top, student_total, teacher_top, teacher_total, teacher_gap = [
        sums[:, i].reshape(sums.shape[0], -1) for i in range(5)
    ]
    top = jnp.max(student_top, axis=0)
    total = jnp.sum(student_total * jnp.exp(student_top - top), axis=0)
    t_top = jnp.max(teacher_top, axis=0)
    t_scale = jnp.exp(teacher_top - t_top)
    t_total = jnp.sum(teacher_total * t_scale, axis=0)
    student_lse = top + jnp.log(total)
    teacher_lse = t_top + jnp.log(t_total)
    kl_row = jnp.sum(teacher_gap * t_scale, axis=0) / t_total - teacher_lse + student_lse
    return student_lse, teacher_lse, kl_row


def solution(mesh):
    return jax.shard_map(
        body,
        mesh=mesh,
        in_specs=(
            P("dp", None),
            P("dp", None),
            P("dp", None),
            P(None, ("dp", "vocab"), None),
            P(None, ("dp", "vocab"), None),
            P(None, ("dp", "vocab")),
            P(("vocab", "dp"), None),
            P(None, ("dp", "vocab"), None),
            P(None, ("dp", "vocab"), None),
            P(None, ("dp", "vocab"), None),
            P(None, ("dp", "vocab"), None),
            P(None, ("dp", "vocab")),
            P(None, ("dp", "vocab")),
            P(("vocab", "dp"), None),
            P(("vocab", "dp"), None),
            P(None, ("dp", "vocab"), None),
            P(None, ("dp", "vocab"), None),
            P(None, ("dp", "vocab")),
            P("vocab", "dp"),
            P("vocab", "dp"),
        ),
        out_specs=(
            P(None, ("dp", "vocab"), None),
            P(None, ("dp", "vocab"), None),
            P(None, ("dp", "vocab"), None),
            P(None, ("dp", "vocab"), None),
            P(None, ("dp", "vocab"), None),
            P(None, ("dp", "vocab"), None),
            P(None, ("dp", "vocab")),
            P(None, ("dp", "vocab")),
            P(None, ("dp", "vocab")),
            P(("vocab", "dp"), None),
            P(("vocab", "dp"), None),
            P(("vocab", "dp"), None),
            P(),
            P(),
            P(),
        ),
        check_vma=False,
    )
```

```python
import jax
import jax.numpy as jnp
from jax import lax
from jax.sharding import PartitionSpec as P

D_S = 512
HDIM = 64
LANES = 128


masked_score = -1000000000.0
beta_one = 0.9
beta_two = 0.99
adam_eps = 1e-10
decay = 0.01
rate = 0.05
clip_at = 0.003
step_count = 10

BF = jnp.bfloat16
F32 = jnp.float32


def swap(value, axis, flip):
    count = lax.axis_size(axis)
    return lax.ppermute(value, axis, [(i, i ^ flip) for i in range(count)])


def trade(blocks, axis):
    return [blocks[0]] + [swap(blocks[k], axis, k) for k in range(1, len(blocks))]


def spread(value, axis):
    return trade([value] * lax.axis_size(axis), axis)


def relative(value, axis, dim=0):
    order = jnp.arange(lax.axis_size(axis)) ^ lax.axis_index(axis)
    return jnp.take(value, order, axis=dim)


def flips(axis):
    count = lax.axis_size(axis)
    bits = count.bit_length() - 1
    return [1 << (bits - 1 - i) for i in range(bits)]


def run(steps):
    got = None
    try:
        while True:
            got = steps.send(got)[0]
    except StopIteration as end:
        return end.value


def adding(value):
    for axis in ("dp", "vocab"):
        for flip in flips(axis)[::-1]:
            value = value + (yield swap(value, axis, flip), 1)
    return value


def sum_everywhere(value):
    return run(adding(value))


def doubling(piece, bits, order):
    held = piece.reshape((1,) * len(bits) + piece.shape)
    for i in order:
        got = yield swap(held, *bits[i]), 1
        high = own_bit(*bits[i]) == 1
        held = jnp.concatenate([jnp.where(high, got, held), jnp.where(high, held, got)], axis=i)
    return held


def pieces_by_xor(piece, axis):
    parts = {0: piece}
    for flip in flips(axis):
        keys = list(parts)
        got = yield [swap(parts[k], axis, flip) for k in keys], 1
        parts.update({k ^ flip: part for k, part in zip(keys, got)})
    return [parts[k] for k in range(len(parts))]


def share_bits():
    return [("dp", flip) for flip in flips("dp")] + [("vocab", flip) for flip in flips("vocab")]


def own_bit(axis, flip):
    return (lax.axis_index(axis) // flip) % 2


def halving(value, bits, order):
    terms = [(value, ())]
    fixed = []
    tail = value.shape[len(bits) :]

    def part(held, since, bit_at):
        start = [0] * value.ndim
        size = list(held.shape)
        for i, bit in bit_at:
            start[i], size[i] = bit, 1
        for i in fixed:
            if i not in since:
                start[i], size[i] = own_bit(*bits[i]), 1
        return lax.dynamic_slice(held, start, size).astype(F32)

    for place, i in enumerate(order):
        sent = sum(part(held, since, [(i, 1 - own_bit(*bits[i]))]) for held, since in terms)
        got = yield swap(sent.astype(BF), *bits[i]), (1, 3, 2, 2)[min(place, 3)]
        fixed.append(i)
        terms.append((got, tuple(fixed)))
    return sum(part(held, since, []) for held, since in terms).reshape(tail)


class Flows:
    def __init__(self):
        self.waiting = []
        self.results = {}

    def begin(self, name, steps):
        self.step(name, steps, None)

    def step(self, name, steps, got):
        try:
            value, turns = steps.send(got)
            self.waiting.append([name, steps, value, turns])
        except StopIteration as end:
            self.results[name] = end.value

    def turn(self, stream=None):
        for flow in self.waiting:
            flow[3] -= 1
        due = [flow for flow in self.waiting if flow[3] <= 0]
        self.waiting = [flow for flow in self.waiting if flow[3] > 0]
        stream, arrived = lax.optimization_barrier((stream, [flow[2] for flow in due]))
        for (name, steps, _, _), got in zip(due, arrived):
            self.step(name, steps, got)
        return stream

    def finish(self):
        while self.waiting:
            self.turn()
        return self.results


def two_orders(bits):
    core = len(flips("dp")) - 1
    first = [i for i in range(core)]
    last = len(bits) - 1
    middle = [i for i in range(core + 1, last)]
    return core, first, middle, last


def reduce_rows(flows, name, grad, turned):
    bits = share_bits()
    shares = 1 << len(bits)
    rows, columns = grad.shape
    grad = grad.reshape((2,) * len(bits) + (rows // shares, columns))
    core, first, middle, last = two_orders(bits)
    order = [core, last] + first + middle if turned else [core] + first + [last] + middle
    flows.begin(name, halving(grad, bits, order))


def project(residual_stream, weight_matrix):
    return jnp.dot(residual_stream, weight_matrix, preferred_element_type=F32)


def project_back(residual_stream, weight_matrix):
    return jnp.einsum("vim,tm->vit", residual_stream, weight_matrix, preferred_element_type=F32)


def outer_sum(left_operand, right_operand):
    return jnp.einsum("uwf,uwp->fp", left_operand, right_operand, preferred_element_type=F32).astype(
        BF
    )


def split_heads(residual_stream):
    return residual_stream.reshape(
        residual_stream.shape[0], residual_stream.shape[1], residual_stream.shape[2] // HDIM, HDIM
    )


def norm_forward(residual_stream, gain_row):
    inverse = lax.rsqrt(jnp.mean(residual_stream * residual_stream, axis=-1, keepdims=True) + 1e-06)
    return (residual_stream * inverse * gain_row.astype(F32), inverse)


def norm_backward(upstream, residual_stream, inverse, gain_row):
    weighted = upstream * gain_row.astype(F32)
    gain_grad = jnp.sum(upstream * residual_stream * inverse, axis=(0, 1))
    stream_grad = inverse * weighted - residual_stream * inverse**3 * jnp.mean(
        weighted * residual_stream, axis=-1, keepdims=True
    )
    return (stream_grad, gain_grad)


def scores_of(query_low, key_low, causal):
    scores = jnp.einsum(
        "sqhd,skhd->shqk",
        split_heads(query_low),
        split_heads(key_low),
        preferred_element_type=F32,
    ) * HDIM ** (-0.5)
    if causal:
        rows_idx = lax.broadcasted_iota(jnp.int32, scores.shape, 2)
        cols_idx = lax.broadcasted_iota(jnp.int32, scores.shape, 3)
        scores = jnp.where(cols_idx <= rows_idx, scores, masked_score)
    return scores


def attend_forward(query_in, key_in, weights, causal):
    width = weights.shape[0]
    if key_in is None:
        joint = project(query_in, weights[:, : 3 * width]).astype(BF)
        query_low = joint[..., :width]
        joint = joint[..., width:]
    else:
        query_low = project(query_in, weights[:, :width]).astype(BF)
        joint = project(key_in, weights[:, width : 3 * width]).astype(BF)
    key_low, value_low = joint[..., :width], joint[..., width:]
    scores = scores_of(query_low, key_low, causal)
    row_top = jnp.max(scores, axis=-1, keepdims=True)
    shifted = jnp.exp(scores - row_top)
    row_total = jnp.sum(shifted, axis=-1, keepdims=True)
    attn_prob = (shifted / row_total).astype(BF)
    log_total = row_top + jnp.log(row_total)
    context = jnp.einsum(
        "shqk,skhd->sqhd", attn_prob, split_heads(value_low), preferred_element_type=F32
    )
    context = context.reshape(query_in.shape[0], query_in.shape[1], -1).astype(BF)
    return (
        project(context, weights[:, 3 * width :]),
        (query_low, key_low, value_low, context, log_total),
    )


def attend_backward(flows, name, output_gradient, query_in, key_in, weights, stored, causal):
    width = weights.shape[0]
    query_low, key_low, value_low, context, log_total = stored
    out_low = output_gradient.astype(BF)
    context_grad = project_back(out_low, weights[:, 3 * width :]).astype(BF)
    context_grad = flows.turn(context_grad)
    attn_prob = jnp.exp(scores_of(query_low, key_low, causal) - log_total)
    prob_grad = jnp.einsum(
        "sqhd,skhd->shqk",
        split_heads(context_grad),
        split_heads(value_low),
        preferred_element_type=F32,
    )
    score_grad = (
        attn_prob * (prob_grad - jnp.sum(attn_prob * prob_grad, axis=-1, keepdims=True))
    ).astype(BF)
    query_grad = (
        (
            jnp.einsum(
                "shqk,skhd->sqhd", score_grad, split_heads(key_low), preferred_element_type=F32
            )
            * HDIM ** (-0.5)
        )
        .reshape(query_low.shape)
        .astype(BF)
    )
    key_grad = (
        (
            jnp.einsum(
                "shqk,sqhd->skhd", score_grad, split_heads(query_low), preferred_element_type=F32
            )
            * HDIM ** (-0.5)
        )
        .reshape(key_low.shape)
        .astype(BF)
    )
    value_grad = (
        jnp.einsum(
            "shqk,sqhd->skhd",
            attn_prob.astype(BF),
            split_heads(context_grad),
            preferred_element_type=F32,
        )
        .reshape(value_low.shape)
        .astype(BF)
    )
    if key_in is None:
        joint = jnp.concatenate([query_grad, key_grad, value_grad], axis=-1)
        weight_grad = [outer_sum(query_in, joint), outer_sum(context, out_low)]
        in_grad = project_back(joint, weights[:, : 3 * width])
        grads = (in_grad, in_grad)
    else:
        joint = jnp.concatenate([key_grad, value_grad], axis=-1)
        weight_grad = [
            outer_sum(query_in, query_grad),
            outer_sum(key_in, joint),
            outer_sum(context, out_low),
        ]
        grads = (
            project_back(query_grad, weights[:, :width]),
            project_back(joint, weights[:, width : 3 * width]),
        )
    grads, weight_grad = flows.turn((grads, weight_grad))
    reduce_rows(flows, name, jnp.concatenate(weight_grad, axis=1), name == "cross")
    return grads


def relu_forward(normed, weight_matrix):
    halfway = weight_matrix.shape[1] // 2
    pre_act = project(normed, weight_matrix[:, :halfway])
    hidden = jnp.maximum(pre_act, 0.0).astype(BF)
    return (project_back(hidden, weight_matrix[:, halfway:]), (pre_act > 0.0, hidden))


def relu_backward(flows, name, output_gradient, normed, weight_matrix, stored):
    positive, hidden = stored
    halfway = weight_matrix.shape[1] // 2
    out_low = output_gradient.astype(BF)
    hidden_grad = project(out_low, weight_matrix[:, halfway:])
    pre_grad = jnp.where(positive, hidden_grad, 0.0).astype(BF)
    weight_grad = [outer_sum(normed, pre_grad), outer_sum(out_low, hidden)]
    normed_grad = project_back(pre_grad, weight_matrix[:, :halfway])
    normed_grad, weight_grad = flows.turn((normed_grad, weight_grad))
    reduce_rows(flows, name, jnp.concatenate(weight_grad, axis=1), name == "enc_ffn")
    return normed_grad


def gated_forward(normed, weight_matrix):
    columns = weight_matrix.shape[1] // 3
    hidden = (
        jax.nn.gelu(project(normed, weight_matrix[:, :columns]), approximate=True)
        * project(normed, weight_matrix[:, columns : 2 * columns])
    ).astype(BF)
    return (project_back(hidden, weight_matrix[:, 2 * columns :]), None)


def encoder_forward(residual_stream, attn, ffn, gains, ffn_forward, turn=lambda stream: stream):
    normed_one, inv_one = norm_forward(residual_stream, gains[0])
    normed_one = normed_one.astype(BF)
    branch, attn_stored = attend_forward(normed_one, None, attn, False)
    stream_one = turn(residual_stream + branch)
    normed_two, inv_two = norm_forward(stream_one, gains[1])
    normed_two = normed_two.astype(BF)
    branch, ffn_stored = ffn_forward(normed_two, ffn)
    stream_two = turn(stream_one + branch)
    result, inv_out = norm_forward(stream_two, gains[2])
    return (
        result.astype(BF),
        (
            inv_one,
            normed_one,
            attn_stored,
            stream_one,
            inv_two,
            normed_two,
            ffn_stored,
            stream_two,
            inv_out,
        ),
    )


def encoder_backward(flows, output_gradient, residual_stream, stored, attn, ffn, gains):
    (
        inv_one,
        normed_one,
        attn_stored,
        stream_one,
        inv_two,
        normed_two,
        ffn_stored,
        stream_two,
        inv_out,
    ) = stored
    grad_two, gain_two = norm_backward(output_gradient, stream_two, inv_out, gains[2])
    normed_grad = relu_backward(flows, "enc_ffn", grad_two, normed_two, ffn, ffn_stored)
    grad_part, gain_one = norm_backward(normed_grad, stream_one, inv_two, gains[1])
    grad_one = grad_two + grad_part
    in_grad, _ = attend_backward(
        flows, "enc", grad_one, normed_one, None, attn, attn_stored, False
    )
    grad_part, gain_zero = norm_backward(in_grad, residual_stream, inv_one, gains[0])
    return (grad_one + grad_part, [gain_zero, gain_one, gain_two])


def decoder_forward(residual_stream, memory, attn, ffn, gains, ffn_forward, out_scale):
    self_attn, cross_attn = attn
    normed_one, inv_one = norm_forward(residual_stream, gains[3])
    normed_one = normed_one.astype(BF)
    branch, self_stored = attend_forward(normed_one, None, self_attn, True)
    stream_one = residual_stream + branch
    normed_two, inv_two = norm_forward(stream_one, gains[4])
    normed_two = normed_two.astype(BF)
    branch, cross_stored = attend_forward(normed_two, memory, cross_attn, False)
    stream_two = stream_one + branch
    normed_three, inv_three = norm_forward(stream_two, gains[5])
    normed_three = normed_three.astype(BF)
    branch, ffn_stored = ffn_forward(normed_three, ffn)
    stream_three = stream_two + branch
    result, inv_out = norm_forward(stream_three, gains[6])
    stored = (
        inv_one,
        normed_one,
        self_stored,
        stream_one,
        inv_two,
        normed_two,
        cross_stored,
        stream_two,
        inv_three,
        normed_three,
        ffn_stored,
        stream_three,
        inv_out,
    )
    return ((result * out_scale).astype(BF), stored)


def decoder_backward(
    flows, output_gradient, residual_stream, memory, stored, attn, ffn, gains, out_scale
):
    (
        inv_one,
        normed_one,
        self_stored,
        stream_one,
        inv_two,
        normed_two,
        cross_stored,
        stream_two,
        inv_three,
        normed_three,
        ffn_stored,
        stream_three,
        inv_out,
    ) = stored
    self_attn, cross_attn = attn
    grad_three, gain_six = norm_backward(
        output_gradient * out_scale, stream_three, inv_out, gains[6]
    )
    normed_grad = relu_backward(flows, "dec_ffn", grad_three, normed_three, ffn, ffn_stored)
    grad_part, gain_five = norm_backward(normed_grad, stream_two, inv_three, gains[5])
    grad_two = grad_three + grad_part
    query_in_grad, memory_grad = attend_backward(
        flows, "cross", grad_two, normed_two, memory, cross_attn, cross_stored, False
    )
    grad_part, gain_four = norm_backward(query_in_grad, stream_one, inv_two, gains[4])
    grad_one = grad_two + grad_part
    in_grad, _ = attend_backward(
        flows, "self", grad_one, normed_one, None, self_attn, self_stored, True
    )
    grad_part, gain_three = norm_backward(in_grad, residual_stream, inv_one, gains[3])
    return (
        grad_one + grad_part,
        memory_grad,
        [gain_three, gain_four, gain_five, gain_six],
    )


class Requests:
    def __init__(self, ids, part_rows, padded_rows):
        members, tokens = ids.shape
        index = lax.axis_index("vocab")
        vocab_rows = part_rows * lax.axis_size("dp")
        self.room = -(-(tokens * 7) // (members * 6 * 16)) * 16
        place = lax.broadcasted_iota(jnp.int32, (1, tokens, tokens), 2)
        same = ids[:, :, None] == ids[:, None, :]
        first = jnp.min(jnp.where(same, place, tokens), axis=2)
        unique = first == jnp.arange(tokens)[None, :]
        shard = ids // vocab_rows
        mine = unique & (shard == index)
        before = (jnp.arange(tokens)[:, None] < jnp.arange(tokens)[None, :]).astype(BF)
        self.place = jnp.dot(mine.astype(BF), before, preferred_element_type=F32).astype(jnp.int32)
        self.mine = mine
        self.local = ids - index * vocab_rows
        self.padded = self.local + self.local // part_rows * (padded_rows - part_rows)
        near = (shard[0][:, None] == shard[0][None, :]) & unique[0][None, :]
        near = near & (place[0] < first[0][:, None])
        self.own_place = jnp.sum(near.astype(jnp.int32), axis=1)
        self.own_shard = shard[0] ^ index
        of_shard = shard[:, :, None] == jnp.arange(members)[None, None, :]
        counts = jnp.sum((of_shard & unique[:, :, None]).astype(jnp.int32), axis=1)
        self.most = jnp.max(counts).reshape(1)

    def counting(self):
        most = self.most
        for flip in flips("dp"):
            most = jnp.maximum(most, (yield swap(most, "dp", flip), 1))
        self.rounds = (most[0] + self.room - 1) // self.room

    def listed(self, turn, padded=True):
        slot = turn * self.room + jnp.arange(self.room)[None, :, None]
        hit = self.mine[:, None, :] & (self.place[:, None, :] == slot)
        rows = (self.padded + 1 if padded else self.local)[:, None, :]
        rows = jnp.sum(jnp.where(hit, rows, 0), axis=2)
        return rows - 1 if padded else rows

    def chosen(self, turn):
        spot = self.own_place - turn * self.room
        inside = (spot >= 0) & (spot < self.room)
        spot = jnp.where(inside, self.own_shard * self.room + spot, -1)
        return (spot[:, None] == jnp.arange(self.mine.shape[0] * self.room)[None, :]).astype(BF)


def take_rows(table, rows):
    return jnp.take(table, rows.reshape(-1), axis=0).reshape(rows.shape + (table.shape[1],))


def chosen_rows(requests, turn, found):
    return jnp.dot(requests.chosen(turn), jnp.concatenate(found), preferred_element_type=F32)


def split_blocks(blocks):
    return [blocks[k] for k in range(blocks.shape[0])]


def student_rows_of(requests, turn, table):
    found = take_rows(table, jnp.maximum(requests.listed(turn), 0))
    found = yield trade(split_blocks(found), "vocab"), 1
    return chosen_rows(requests, turn, found)


def teacher_rows_of(requests, turn, column_part):
    asked = yield spread(requests.listed(turn, False), "dp"), 1
    found = yield trade([take_rows(column_part, rows) for rows in asked], "dp"), 1
    found = yield trade(split_blocks(jnp.stack(found, axis=2)), "vocab"), 1
    found = relative(jnp.concatenate(found), "dp", 1)
    return chosen_rows(requests, turn, [found.reshape(found.shape[0], -1)])


def table_grad_of(requests, turn, embed_grad, padded_rows):
    rows = requests.listed(turn)
    wanted = jnp.einsum("tr,td->rd", requests.chosen(turn), embed_grad, preferred_element_type=F32)
    wanted = wanted.astype(BF).reshape(rows.shape + (embed_grad.shape[1],))
    got = yield trade(split_blocks(wanted), "vocab"), 1
    got_parts, row_parts = [jnp.concatenate(got)], [rows.reshape(1, -1)]
    for flip in flips("dp"):
        got = yield [[swap(part, "dp", flip) for part in parts] for parts in (got_parts, row_parts)], 1
        got_parts, row_parts = got_parts + got[0], row_parts + got[1]
    own = lax.axis_index("dp") * padded_rows + jnp.arange(padded_rows)[:, None]
    return sum(
        jnp.dot((own == rows).astype(BF), part, preferred_element_type=F32)
        for part, rows in zip(got_parts, row_parts)
    )


def all_rounds(requests, start, one_round):
    def more(state):
        return state[0] < requests.rounds

    def again(state):
        return state[0] + 1, state[1] + one_round(state[0])

    return lax.while_loop(more, again, (jnp.int32(1), start))[1]


def moments(grad_part, first_part, second_part, master):
    new_first = beta_one * first_part + (1.0 - beta_one) * grad_part
    new_second = beta_two * second_part + (1.0 - beta_two) * grad_part * grad_part
    direction = (
        new_first
        / (1.0 - beta_one**step_count)
        / (jnp.sqrt(new_second / (1.0 - beta_two**step_count)) + adam_eps)
        + decay * master
    )
    return (new_first, new_second, direction)


def tensor_sums(arrays):
    attn, ffn, gains, table = arrays
    halfway = ffn.shape[2] // 2
    ffn_parts = jnp.stack(
        [
            jnp.sum(ffn[:, :, :halfway] ** 2, axis=(1, 2)),
            jnp.sum(ffn[:, :, halfway:] ** 2, axis=(1, 2)),
        ],
        axis=1,
    ).reshape(-1)
    return jnp.concatenate(
        [
            jnp.sum(attn * attn, axis=(1, 2)),
            ffn_parts,
            jnp.sum(gains * gains, axis=1),
            jnp.sum(table * table).reshape(1),
        ]
    )


def expand_ratios(ratio, halfway):
    ffn_ratio = jnp.repeat(ratio[12:16].reshape(2, 2), halfway, axis=1)[:, None, :]
    return (ratio[:12][:, None, None], ffn_ratio, ratio[16:23][:, None], ratio[23])


def side_by_side(matrices):
    return matrices.transpose(1, 0, 2).reshape(matrices.shape[1], -1)


def gather_rows(pieces):
    return lax.all_gather(jnp.concatenate(pieces, axis=1), ("dp", "vocab"), axis=0, tiled=True)


def gain_columns(gains):
    return jnp.pad(gains.T, ((0, 0), (0, LANES - gains.shape[0])))


def body(
    enc_ids,
    dec_ids,
    dec_mask,
    s_attn,
    s_ffn,
    s_gains,
    s_table,
    s_attn_m,
    s_attn_v,
    s_ffn_m,
    s_ffn_v,
    s_gains_m,
    s_gains_v,
    s_table_m,
    s_table_v,
    t_attn,
    t_ffn,
    t_gains,
    t_embed,
    t_head,
):
    vocab_count = lax.axis_size("vocab")
    dp_count = lax.axis_size("dp")
    vocab_index = lax.axis_index("vocab")
    seqs = enc_ids.shape[0]
    seq_dev = seqs // vocab_count
    enc_len = enc_ids.shape[1]
    dec_len = dec_ids.shape[1]
    total_seqs = seqs * dp_count
    width = s_attn.shape[2]
    t_width = t_attn.shape[2]
    ffn_width = s_ffn.shape[2]
    gain_count = s_gains.shape[0]
    out_scale = D_S ** (-0.5)

    teacher = gather_rows([side_by_side(t_attn), t_ffn[0], gain_columns(t_gains)])
    teacher_last = gather_rows([t_ffn[1]])
    low_attn, low_ffn = side_by_side(s_attn.astype(BF)), s_ffn.astype(BF)
    enc_pack = [low_attn[:, : 4 * width], low_ffn[0], gain_columns(s_gains.astype(BF))]
    dec_pack = [low_attn[:, 4 * width :], low_ffn[1]]
    bits = share_bits()
    core, first, middle, last = two_orders(bits)
    flows = Flows()
    order = middle + first + [last, core]
    flows.begin("enc", doubling(jnp.concatenate(enc_pack, axis=1), bits, order))
    order = middle + [last] + first + [core]
    flows.begin("dec", doubling(jnp.concatenate(dec_pack, axis=1), bits, order))

    part_rows = s_table.shape[0]
    padded_rows = -(-part_rows // LANES) * LANES
    padding = ((0, padded_rows - part_rows), (0, 0))
    dp_bits = [("dp", flip) for flip in flips("dp")]
    dp_order = list(range(len(dp_bits)))
    flows.begin("table", doubling(jnp.pad(s_table.astype(BF), padding), dp_bits, dp_order))
    part_columns = t_head.shape[1]
    head_part = t_head.reshape(dp_count, part_rows, part_columns)
    head_part = jnp.pad(head_part, ((0, 0),) + padding).reshape(-1, part_columns)
    in_use = jnp.arange(dp_count * padded_rows)[None, :] % padded_rows < part_rows
    ids = jnp.concatenate(
        [enc_ids.reshape(vocab_count, -1), dec_ids.reshape(vocab_count, -1)], axis=1
    )
    requests = Requests(relative(ids, "vocab"), part_rows, padded_rows)
    flows.begin("count", requests.counting())
    flows.begin("t_rows", teacher_rows_of(requests, jnp.int32(0), t_embed))
    while "table" not in flows.results:
        flows.turn()
    table = flows.results["table"].reshape(-1, width)
    flows.begin("rows", student_rows_of(requests, jnp.int32(0), table))
    while not {"rows", "t_rows"} <= flows.results.keys():
        flows.turn()

    def student_round(turn):
        return run(student_rows_of(requests, turn, table))

    def teacher_round(turn):
        return run(teacher_rows_of(requests, turn, t_embed))

    embedded = all_rounds(requests, flows.results["rows"], student_round)
    t_embedded = all_rounds(requests, flows.results["t_rows"], teacher_round)
    enc_tokens = seq_dev * enc_len

    def parted(rows):
        return (
            rows[:enc_tokens].reshape(seq_dev, enc_len, -1),
            rows[enc_tokens:].reshape(seq_dev, dec_len, -1),
        )

    enc_in, dec_in = parted(embedded)
    t_enc_in, t_dec_in = parted(t_embedded)

    cut = 4 * t_width
    tattn = [teacher[:, i * cut : (i + 1) * cut] for i in range(3)]
    tffn = teacher[:, 3 * cut : 3 * cut + t_ffn.shape[2]]
    tgains = teacher[:, 3 * cut + t_ffn.shape[2] :].T[:gain_count]
    t_memory, _ = encoder_forward(
        t_enc_in, tattn[0], tffn, tgains, gated_forward, turn=flows.turn
    )
    flows.finish()
    student_enc, student_dec = [
        flows.results[name].reshape(width, -1) for name in ("enc", "dec")
    ]
    flows.begin("head", pieces_by_xor(head_part, "dp"))

    cut = 4 * width
    attn = [student_enc[:, :cut], student_dec[:, :cut], student_dec[:, cut : 2 * cut]]
    ffn = [student_enc[:, cut : cut + ffn_width], student_dec[:, 2 * cut :]]
    gains = student_enc[:, cut + ffn_width :].T[:gain_count]
    enc_in, t_memory = lax.optimization_barrier((enc_in, t_memory))
    memory, enc_stored = encoder_forward(enc_in, attn[0], ffn[0], gains, relu_forward)
    memory = flows.turn(memory)
    head_in, dec_stored = decoder_forward(
        dec_in, memory, attn[1:], ffn[1], gains, relu_forward, out_scale
    )
    student_rows = spread(head_in.reshape(-1, width), "vocab")
    t_dec_in, head_in = lax.optimization_barrier((t_dec_in, head_in))
    t_dec_in = flows.turn(t_dec_in)

    thead = jnp.concatenate(flows.finish()["head"], axis=1)

    t_head_in, _ = decoder_forward(
        t_dec_in, t_memory, tattn[1:], teacher_last, tgains, gated_forward, 1.0
    )
    t_head_rows = relative(t_head_in.reshape(-1, dp_count, part_columns), "dp", 1)
    t_head_rows = t_head_rows.reshape(-1, t_width)
    early = vocab_count // 4
    student_rows[early:], t_head_rows = lax.optimization_barrier(
        (student_rows[early:], t_head_rows)
    )
    teacher_rows = spread(t_head_rows, "vocab")
    student_logit = [head_logits(rows, table, in_use) for rows in student_rows]
    student_sums = [logit_sums(logit) for logit in student_logit]
    teacher_logit = [head_logits(rows, thead, in_use) for rows in teacher_rows]
    teacher_sums = [logit_sums(*logits) for logits in zip(teacher_logit, student_logit)]

    own_rows = seq_dev * dec_len
    sums = jnp.stack(
        [
            jnp.stack(student[:2] + teacher[:3])
            for student, teacher in zip(student_sums, teacher_sums)
        ],
        axis=1,
    )
    own_tops = sums[0], sums[2]
    for flip in flips("vocab")[::-1]:
        other = swap(sums, "vocab", flip)
        sums = merge_sums(sums, jnp.stack([other[:, i ^ flip] for i in range(vocab_count)], axis=1))
    student_lse = sums[0] + jnp.log(sums[1])
    teacher_lse = sums[2] + jnp.log(sums[3])
    kl_row = sums[4] / sums[3] - teacher_lse + student_lse
    end_mask = relative(dec_mask.astype(F32).reshape(vocab_count, seq_dev, dec_len), "vocab")
    row_weight = end_mask / (jnp.sum(end_mask, axis=2, keepdims=True) * total_seqs)
    row_weight = row_weight.reshape(vocab_count, own_rows)
    loss_sum = jnp.sum(row_weight[0] * kl_row[0])
    student_scale = row_weight * jnp.exp(own_tops[0] - student_lse)
    teacher_scale = row_weight * jnp.exp(own_tops[1] - teacher_lse)
    logit_grad = [
        (
            student_scale[k][:, None] * student_sums[k][-1].astype(F32)
            - teacher_scale[k][:, None] * teacher_sums[k][-1].astype(F32)
        ).astype(BF)
        for k in range(vocab_count)
    ]
    head_parts = [
        jnp.dot(grad, table, preferred_element_type=F32).astype(BF) for grad in logit_grad
    ]
    head_parts = trade(head_parts, "vocab")
    table_grad = lax.dot_general(
        jnp.concatenate(logit_grad),
        jnp.concatenate(student_rows),
        (((0,), (0,)), ((), ())),
        preferred_element_type=F32,
    ).astype(BF)
    head_parts, table_grad = lax.optimization_barrier((head_parts, table_grad))
    head_grad = sum(part.astype(F32) for part in head_parts).reshape(head_in.shape)
    flows = Flows()
    table_grad = table_grad.reshape((2,) * len(dp_bits) + (padded_rows, width))
    flows.begin("table", halving(table_grad, dp_bits, dp_order[::-1]))

    dec_in_grad, memory_grad, dec_gains = decoder_backward(
        flows, head_grad, dec_in, memory, dec_stored, attn[1:], ffn[1], gains, out_scale
    )
    enc_in_grad, enc_gains = encoder_backward(
        flows, memory_grad, enc_in, enc_stored, attn[0], ffn[0], gains
    )
    embed_grad = jnp.concatenate(
        [enc_in_grad.reshape(-1, width), dec_in_grad.reshape(-1, width)]
    ).astype(BF)

    flows.begin("rows", table_grad_of(requests, jnp.int32(0), embed_grad, padded_rows))
    flows.begin("gains", adding(jnp.stack(enc_gains + dec_gains)))
    owned = flows.finish()

    def grad_round(turn):
        return run(table_grad_of(requests, turn, embed_grad, padded_rows))

    table_grad = all_rounds(requests, owned["table"] + owned["rows"], grad_round)
    table_shard = table_grad[:part_rows]
    gain_sums = owned["gains"]
    share = lax.axis_index("dp") * vocab_count + vocab_index
    gains_shard = lax.dynamic_slice_in_dim(gain_sums, share * s_gains.shape[1], s_gains.shape[1], 1)

    def stacked(matrix):
        return matrix.reshape(matrix.shape[0], -1, width).transpose(1, 0, 2)

    attn_shard = jnp.concatenate(
        [stacked(owned[name]) for name in ("enc", "self", "cross")]
    )
    ffn_shard = jnp.stack([owned["enc_ffn"], owned["dec_ffn"]])

    gradients = (attn_shard, ffn_shard, gains_shard, table_shard)
    masters = (s_attn, s_ffn, s_gains, s_table)
    square_sum = sum((jnp.sum(part * part) for part in gradients))
    totals = jnp.concatenate([jnp.stack([square_sum, loss_sum]), tensor_sums(masters)])
    totals = sum_everywhere(totals)
    grad_norm = jnp.sqrt(totals[0])
    loss = totals[1]
    factor = jnp.minimum(1.0, clip_at / grad_norm)
    firsts = (s_attn_m, s_ffn_m, s_gains_m, s_table_m)
    seconds = (s_attn_v, s_ffn_v, s_gains_v, s_table_v)
    states = [
        moments(grad_part * factor, first_part, second_part, master)
        for grad_part, first_part, second_part, master in zip(gradients, firsts, seconds, masters)
    ]
    directions = tuple((state[2] for state in states))
    tensor_norm = jnp.sqrt(jnp.stack([totals[2:], sum_everywhere(tensor_sums(directions))]))
    ratio = tensor_norm[0] / (tensor_norm[1] + 1e-06)
    expanded = expand_ratios(ratio, s_ffn.shape[2] // 2)
    updates = [-rate * scale_part * state[2] for scale_part, state in zip(expanded, states)]
    return (
        states[0][0],
        states[0][1],
        updates[0],
        states[1][0],
        states[1][1],
        updates[1],
        states[2][0],
        states[2][1],
        updates[2],
        states[3][0],
        states[3][1],
        updates[3],
        tensor_norm,
        grad_norm,
        loss,
    )


def head_logits(rows, head, in_use):
    logit = lax.dot_general(rows, head, (((1,), (1,)), ((), ())), preferred_element_type=F32)
    return jnp.where(in_use, logit, masked_score)


def logit_sums(logit, other=None):
    top = jnp.max(logit, axis=1)
    weight = jnp.exp(logit - top[:, None])
    sums = [top, jnp.sum(weight, axis=1)]
    if other is not None:
        sums.append(jnp.sum(weight * (logit - other), axis=1))
    return sums + [lax.optimization_barrier(weight.astype(BF))]


def merge_sums(one, two):
    top = jnp.maximum(one[0], two[0])
    t_top = jnp.maximum(one[2], two[2])
    scale_one, scale_two = jnp.exp(one[2] - t_top), jnp.exp(two[2] - t_top)
    return jnp.stack(
        [
            top,
            one[1] * jnp.exp(one[0] - top) + two[1] * jnp.exp(two[0] - top),
            t_top,
            one[3] * scale_one + two[3] * scale_two,
            one[4] * scale_one + two[4] * scale_two,
        ]
    )


def solution(mesh):
    return jax.shard_map(
        body,
        mesh=mesh,
        in_specs=(
            P("dp", None),
            P("dp", None),
            P("dp", None),
            P(None, ("dp", "vocab"), None),
            P(None, ("dp", "vocab"), None),
            P(None, ("dp", "vocab")),
            P(("vocab", "dp"), None),
            P(None, ("dp", "vocab"), None),
            P(None, ("dp", "vocab"), None),
            P(None, ("dp", "vocab"), None),
            P(None, ("dp", "vocab"), None),
            P(None, ("dp", "vocab")),
            P(None, ("dp", "vocab")),
            P(("vocab", "dp"), None),
            P(("vocab", "dp"), None),
            P(None, ("dp", "vocab"), None),
            P(None, ("dp", "vocab"), None),
            P(None, ("dp", "vocab")),
            P("vocab", "dp"),
            P("vocab", "dp"),
        ),
        out_specs=(
            P(None, ("dp", "vocab"), None),
            P(None, ("dp", "vocab"), None),
            P(None, ("dp", "vocab"), None),
            P(None, ("dp", "vocab"), None),
            P(None, ("dp", "vocab"), None),
            P(None, ("dp", "vocab"), None),
            P(None, ("dp", "vocab")),
            P(None, ("dp", "vocab")),
            P(None, ("dp", "vocab")),
            P(("vocab", "dp"), None),
            P(("vocab", "dp"), None),
            P(("vocab", "dp"), None),
            P(),
            P(),
            P(),
        ),
        check_vma=False,
    )
```

```python
import jax
import jax.numpy as jnp
from jax import lax
from jax.sharding import PartitionSpec as P

D_S = 512
HDIM = 64
LANES = 128
GATHER_AFTER = 2


masked_score = -1000000000.0
beta_one = 0.9
beta_two = 0.99
adam_eps = 1e-10
decay = 0.01
rate = 0.05
clip_at = 0.003
step_count = 10

BF = jnp.bfloat16
F32 = jnp.float32


def swap(value, axis, flip):
    count = lax.axis_size(axis)
    return lax.ppermute(value, axis, [(i, i ^ flip) for i in range(count)])


def trade(blocks, axis):
    return [blocks[0]] + [swap(blocks[k], axis, k) for k in range(1, len(blocks))]


def spread(value, axis):
    return trade([value] * lax.axis_size(axis), axis)


def relative(value, axis, dim=0):
    order = jnp.arange(lax.axis_size(axis)) ^ lax.axis_index(axis)
    return jnp.take(value, order, axis=dim, mode="clip")


def flips(axis):
    count = lax.axis_size(axis)
    bits = count.bit_length() - 1
    return [1 << (bits - 1 - i) for i in range(bits)]


def run(steps):
    got = None
    try:
        while True:
            got = steps.send(got)[0]
    except StopIteration as end:
        return end.value


def adding(value):
    for axis in ("dp", "vocab"):
        for flip in flips(axis)[::-1]:
            value = value + (yield swap(value, axis, flip), 1)
    return value


def sum_everywhere(value):
    return run(adding(value))


def doubling(piece, bits, order):
    held = piece.reshape((1,) * len(bits) + piece.shape)
    for i in order:
        got = yield swap(held, *bits[i]), 1
        high = own_bit(*bits[i]) == 1
        held = jnp.concatenate([jnp.where(high, got, held), jnp.where(high, held, got)], axis=i)
    return held


def pieces_by_xor(piece, axis):
    parts = {0: piece}
    for flip in flips(axis):
        keys = list(parts)
        got = yield [swap(parts[k], axis, flip) for k in keys], 1
        parts.update({k ^ flip: part for k, part in zip(keys, got)})
    return [parts[k] for k in range(len(parts))]


def share_bits():
    return [("dp", flip) for flip in flips("dp")] + [("vocab", flip) for flip in flips("vocab")]


def own_bit(axis, flip):
    return (lax.axis_index(axis) // flip) % 2


def halving(value, bits, order):
    terms = [(value, ())]
    fixed = []
    tail = value.shape[len(bits) :]

    def part(held, since, bit_at):
        start = [0] * value.ndim
        size = list(held.shape)
        for i, bit in bit_at:
            start[i], size[i] = bit, 1
        for i in fixed:
            if i not in since:
                start[i], size[i] = own_bit(*bits[i]), 1
        return lax.dynamic_slice(held, start, size).astype(F32)

    for place, i in enumerate(order):
        sent = sum(part(held, since, [(i, 1 - own_bit(*bits[i]))]) for held, since in terms)
        got = yield swap(sent.astype(BF), *bits[i]), (1, 3, 2, 2)[min(place, 3)]
        fixed.append(i)
        terms.append((got, tuple(fixed)))
    return sum(part(held, since, []) for held, since in terms).reshape(tail)


class Flows:
    def __init__(self):
        self.waiting = []
        self.results = {}

    def begin(self, name, steps):
        self.step(name, steps, None)

    def step(self, name, steps, got):
        try:
            value, turns = steps.send(got)
            self.waiting.append([name, steps, value, turns])
        except StopIteration as end:
            self.results[name] = end.value

    def turn(self, stream=None):
        for flow in self.waiting:
            flow[3] -= 1
        due = [flow for flow in self.waiting if flow[3] <= 0]
        self.waiting = [flow for flow in self.waiting if flow[3] > 0]
        stream, arrived = lax.optimization_barrier((stream, [flow[2] for flow in due]))
        for (name, steps, _, _), got in zip(due, arrived):
            self.step(name, steps, got)
        return stream

    def finish(self):
        while self.waiting:
            self.turn()
        return self.results


def two_orders(bits):
    core = len(flips("dp")) - 1
    first = [i for i in range(core)]
    last = len(bits) - 1
    middle = [i for i in range(core + 1, last)]
    return core, first, middle, last


def reduce_rows(flows, name, grad, turned):
    bits = share_bits()
    shares = 1 << len(bits)
    rows, columns = grad.shape
    grad = grad.reshape((2,) * len(bits) + (rows // shares, columns))
    core, first, middle, last = two_orders(bits)
    order = [core, last] + first + middle if turned else [core] + first + [last] + middle
    flows.begin(name, halving(grad, bits, order))


def project(residual_stream, weight_matrix):
    return jnp.dot(residual_stream, weight_matrix, preferred_element_type=F32)


def project_back(residual_stream, weight_matrix):
    return jnp.einsum("vim,tm->vit", residual_stream, weight_matrix, preferred_element_type=F32)


def outer_sum(left_operand, right_operand):
    return jnp.einsum("uwf,uwp->fp", left_operand, right_operand, preferred_element_type=F32).astype(
        BF
    )


def split_heads(residual_stream):
    return residual_stream.reshape(
        residual_stream.shape[0], residual_stream.shape[1], residual_stream.shape[2] // HDIM, HDIM
    )


def norm_forward(residual_stream, gain_row):
    inverse = lax.rsqrt(jnp.mean(residual_stream * residual_stream, axis=-1, keepdims=True) + 1e-06)
    return (residual_stream * inverse * gain_row.astype(F32), inverse)


def norm_backward(upstream, residual_stream, inverse, gain_row):
    weighted = upstream * gain_row.astype(F32)
    gain_grad = jnp.sum(upstream * residual_stream * inverse, axis=(0, 1))
    stream_grad = inverse * weighted - residual_stream * inverse**3 * jnp.mean(
        weighted * residual_stream, axis=-1, keepdims=True
    )
    return (stream_grad, gain_grad)


def scores_of(query_low, key_low, causal):
    scores = jnp.einsum(
        "sqhd,skhd->shqk",
        split_heads(query_low),
        split_heads(key_low),
        preferred_element_type=F32,
    ) * HDIM ** (-0.5)
    if causal:
        rows_idx = lax.broadcasted_iota(jnp.int32, scores.shape, 2)
        cols_idx = lax.broadcasted_iota(jnp.int32, scores.shape, 3)
        scores = jnp.where(cols_idx <= rows_idx, scores, masked_score)
    return scores


def attend_forward(query_in, key_in, weights, causal):
    width = weights.shape[0]
    if key_in is None:
        joint = project(query_in, weights[:, : 3 * width]).astype(BF)
        query_low = joint[..., :width]
        joint = joint[..., width:]
    else:
        query_low = project(query_in, weights[:, :width]).astype(BF)
        joint = project(key_in, weights[:, width : 3 * width]).astype(BF)
    key_low, value_low = joint[..., :width], joint[..., width:]
    scores = scores_of(query_low, key_low, causal)
    row_top = jnp.max(scores, axis=-1, keepdims=True)
    shifted = jnp.exp(scores - row_top)
    row_total = jnp.sum(shifted, axis=-1, keepdims=True)
    attn_prob = (shifted / row_total).astype(BF)
    log_total = row_top + jnp.log(row_total)
    context = jnp.einsum(
        "shqk,skhd->sqhd", attn_prob, split_heads(value_low), preferred_element_type=F32
    )
    context = context.reshape(query_in.shape[0], query_in.shape[1], -1).astype(BF)
    return (
        project(context, weights[:, 3 * width :]),
        (query_low, key_low, value_low, context, log_total),
    )


def attend_backward(flows, name, output_gradient, query_in, key_in, weights, stored, causal):
    width = weights.shape[0]
    query_low, key_low, value_low, context, log_total = stored
    out_low = output_gradient.astype(BF)
    context_grad = project_back(out_low, weights[:, 3 * width :]).astype(BF)
    context_grad = flows.turn(context_grad)
    attn_prob = jnp.exp(scores_of(query_low, key_low, causal) - log_total)
    prob_grad = jnp.einsum(
        "sqhd,skhd->shqk",
        split_heads(context_grad),
        split_heads(value_low),
        preferred_element_type=F32,
    )
    score_grad = (
        attn_prob * (prob_grad - jnp.sum(attn_prob * prob_grad, axis=-1, keepdims=True))
    ).astype(BF)
    query_grad = (
        (
            jnp.einsum(
                "shqk,skhd->sqhd", score_grad, split_heads(key_low), preferred_element_type=F32
            )
            * HDIM ** (-0.5)
        )
        .reshape(query_low.shape)
        .astype(BF)
    )
    key_grad = (
        (
            jnp.einsum(
                "shqk,sqhd->skhd", score_grad, split_heads(query_low), preferred_element_type=F32
            )
            * HDIM ** (-0.5)
        )
        .reshape(key_low.shape)
        .astype(BF)
    )
    value_grad = (
        jnp.einsum(
            "shqk,sqhd->skhd",
            attn_prob.astype(BF),
            split_heads(context_grad),
            preferred_element_type=F32,
        )
        .reshape(value_low.shape)
        .astype(BF)
    )
    if key_in is None:
        joint = jnp.concatenate([query_grad, key_grad, value_grad], axis=-1)
        weight_grad = [outer_sum(query_in, joint), outer_sum(context, out_low)]
        in_grad = project_back(joint, weights[:, : 3 * width])
        grads = (in_grad, in_grad)
    else:
        joint = jnp.concatenate([key_grad, value_grad], axis=-1)
        weight_grad = [
            outer_sum(query_in, query_grad),
            outer_sum(key_in, joint),
            outer_sum(context, out_low),
        ]
        grads = (
            project_back(query_grad, weights[:, :width]),
            project_back(joint, weights[:, width : 3 * width]),
        )
    grads, weight_grad = flows.turn((grads, weight_grad))
    reduce_rows(flows, name, jnp.concatenate(weight_grad, axis=1), name == "cross")
    return grads


def relu_forward(normed, weight_matrix):
    halfway = weight_matrix.shape[1] // 2
    pre_act = project(normed, weight_matrix[:, :halfway])
    hidden = jnp.maximum(pre_act, 0.0).astype(BF)
    return (project_back(hidden, weight_matrix[:, halfway:]), (pre_act > 0.0, hidden))


def relu_backward(flows, name, output_gradient, normed, weight_matrix, stored):
    positive, hidden = stored
    halfway = weight_matrix.shape[1] // 2
    out_low = output_gradient.astype(BF)
    hidden_grad = project(out_low, weight_matrix[:, halfway:])
    pre_grad = jnp.where(positive, hidden_grad, 0.0).astype(BF)
    weight_grad = [outer_sum(normed, pre_grad), outer_sum(out_low, hidden)]
    normed_grad = project_back(pre_grad, weight_matrix[:, :halfway])
    normed_grad, weight_grad = flows.turn((normed_grad, weight_grad))
    reduce_rows(flows, name, jnp.concatenate(weight_grad, axis=1), name == "enc_ffn")
    return normed_grad


def gated_forward(normed, weight_matrix):
    columns = weight_matrix.shape[1] // 3
    hidden = (
        jax.nn.gelu(project(normed, weight_matrix[:, :columns]), approximate=True)
        * project(normed, weight_matrix[:, columns : 2 * columns])
    ).astype(BF)
    return (project_back(hidden, weight_matrix[:, 2 * columns :]), None)


def encoder_forward(residual_stream, attn, ffn, gains, ffn_forward):
    normed_one, inv_one = norm_forward(residual_stream, gains[0])
    normed_one = normed_one.astype(BF)
    branch, attn_stored = attend_forward(normed_one, None, attn, False)
    stream_one = residual_stream + branch
    normed_two, inv_two = norm_forward(stream_one, gains[1])
    normed_two = normed_two.astype(BF)
    branch, ffn_stored = ffn_forward(normed_two, ffn)
    stream_two = stream_one + branch
    result, inv_out = norm_forward(stream_two, gains[2])
    return (
        result.astype(BF),
        (
            inv_one,
            normed_one,
            attn_stored,
            stream_one,
            inv_two,
            normed_two,
            ffn_stored,
            stream_two,
            inv_out,
        ),
    )


def encoder_backward(flows, output_gradient, residual_stream, stored, attn, ffn, gains):
    (
        inv_one,
        normed_one,
        attn_stored,
        stream_one,
        inv_two,
        normed_two,
        ffn_stored,
        stream_two,
        inv_out,
    ) = stored
    grad_two, gain_two = norm_backward(output_gradient, stream_two, inv_out, gains[2])
    normed_grad = relu_backward(flows, "enc_ffn", grad_two, normed_two, ffn, ffn_stored)
    grad_part, gain_one = norm_backward(normed_grad, stream_one, inv_two, gains[1])
    grad_one = grad_two + grad_part
    in_grad, _ = attend_backward(
        flows, "enc", grad_one, normed_one, None, attn, attn_stored, False
    )
    grad_part, gain_zero = norm_backward(in_grad, residual_stream, inv_one, gains[0])
    return (grad_one + grad_part, [gain_zero, gain_one, gain_two])


def decoder_forward(residual_stream, memory, attn, ffn, gains, ffn_forward, out_scale):
    self_attn, cross_attn = attn
    normed_one, inv_one = norm_forward(residual_stream, gains[3])
    normed_one = normed_one.astype(BF)
    branch, self_stored = attend_forward(normed_one, None, self_attn, True)
    stream_one = residual_stream + branch
    normed_two, inv_two = norm_forward(stream_one, gains[4])
    normed_two = normed_two.astype(BF)
    branch, cross_stored = attend_forward(normed_two, memory, cross_attn, False)
    stream_two = stream_one + branch
    normed_three, inv_three = norm_forward(stream_two, gains[5])
    normed_three = normed_three.astype(BF)
    branch, ffn_stored = ffn_forward(normed_three, ffn)
    stream_three = stream_two + branch
    result, inv_out = norm_forward(stream_three, gains[6])
    stored = (
        inv_one,
        normed_one,
        self_stored,
        stream_one,
        inv_two,
        normed_two,
        cross_stored,
        stream_two,
        inv_three,
        normed_three,
        ffn_stored,
        stream_three,
        inv_out,
    )
    return ((result * out_scale).astype(BF), stored)


def decoder_backward(
    flows, output_gradient, residual_stream, memory, stored, attn, ffn, gains, out_scale
):
    (
        inv_one,
        normed_one,
        self_stored,
        stream_one,
        inv_two,
        normed_two,
        cross_stored,
        stream_two,
        inv_three,
        normed_three,
        ffn_stored,
        stream_three,
        inv_out,
    ) = stored
    self_attn, cross_attn = attn
    grad_three, gain_six = norm_backward(
        output_gradient * out_scale, stream_three, inv_out, gains[6]
    )
    normed_grad = relu_backward(flows, "dec_ffn", grad_three, normed_three, ffn, ffn_stored)
    grad_part, gain_five = norm_backward(normed_grad, stream_two, inv_three, gains[5])
    grad_two = grad_three + grad_part
    query_in_grad, memory_grad = attend_backward(
        flows, "cross", grad_two, normed_two, memory, cross_attn, cross_stored, False
    )
    grad_part, gain_four = norm_backward(query_in_grad, stream_one, inv_two, gains[4])
    grad_one = grad_two + grad_part
    in_grad, _ = attend_backward(
        flows, "self", grad_one, normed_one, None, self_attn, self_stored, True
    )
    grad_part, gain_three = norm_backward(in_grad, residual_stream, inv_one, gains[3])
    return (
        grad_one + grad_part,
        memory_grad,
        [gain_three, gain_four, gain_five, gain_six],
    )


class Requests:
    def __init__(self, ids, part_rows, padded_rows):
        members, tokens = ids.shape
        index = lax.axis_index("vocab")
        vocab_rows = part_rows * lax.axis_size("dp")
        self.room = -(-(tokens * 7) // (members * 6 * 16)) * 16
        place = lax.broadcasted_iota(jnp.int32, (1, tokens, tokens), 2)
        same = ids[:, :, None] == ids[:, None, :]
        first = jnp.min(jnp.where(same, place, tokens), axis=2)
        unique = first == jnp.arange(tokens)[None, :]
        shard = ids // vocab_rows
        mine = unique & (shard == index)
        before = (jnp.arange(tokens)[:, None] < jnp.arange(tokens)[None, :]).astype(BF)
        self.place = jnp.dot(mine.astype(BF), before, preferred_element_type=F32).astype(jnp.int32)
        self.mine = mine
        self.local = ids - index * vocab_rows
        self.padded = self.local + self.local // part_rows * (padded_rows - part_rows)
        near = (shard[0][:, None] == shard[0][None, :]) & unique[0][None, :]
        near = near & (place[0] < first[0][:, None])
        self.own_place = jnp.sum(near.astype(jnp.int32), axis=1)
        self.own_shard = shard[0] ^ index
        of_shard = shard[:, :, None] == jnp.arange(members)[None, None, :]
        counts = jnp.sum((of_shard & unique[:, :, None]).astype(jnp.int32), axis=1)
        self.most = jnp.max(counts).reshape(1)

    def counting(self):
        most = self.most
        for flip in flips("dp"):
            most = jnp.maximum(most, (yield swap(most, "dp", flip), 1))
        self.rounds = (most[0] + self.room - 1) // self.room

    def listed(self, turn, padded=True):
        slot = turn * self.room + jnp.arange(self.room)[None, :, None]
        hit = self.mine[:, None, :] & (self.place[:, None, :] == slot)
        rows = (self.padded + 1 if padded else self.local)[:, None, :]
        rows = jnp.sum(jnp.where(hit, rows, 0), axis=2)
        return rows - 1 if padded else rows

    def chosen(self, turn):
        spot = self.own_place - turn * self.room
        inside = (spot >= 0) & (spot < self.room)
        spot = jnp.where(inside, self.own_shard * self.room + spot, -1)
        return (spot[:, None] == jnp.arange(self.mine.shape[0] * self.room)[None, :]).astype(BF)


def take_rows(table, rows):
    return jnp.take(table, rows.reshape(-1), axis=0, mode="clip").reshape(rows.shape + (table.shape[1],))


def chosen_rows(requests, turn, found):
    return jnp.dot(requests.chosen(turn), jnp.concatenate(found), preferred_element_type=F32)


def split_blocks(blocks):
    return [blocks[k] for k in range(blocks.shape[0])]


def student_rows_of(requests, turn, table):
    found = take_rows(table, jnp.maximum(requests.listed(turn), 0))
    found = yield trade(split_blocks(found), "vocab"), 1
    return chosen_rows(requests, turn, found)


def teacher_rows_of(requests, turn, column_part):
    asked = yield spread(requests.listed(turn, False), "dp"), 1
    found = yield trade([take_rows(column_part, rows) for rows in asked], "dp"), 1
    found = yield trade(split_blocks(jnp.stack(found, axis=2)), "vocab"), 1
    found = relative(jnp.concatenate(found), "dp", 1)
    return chosen_rows(requests, turn, [found.reshape(found.shape[0], -1)])


def joined_dp(value, dim):
    for flip in flips("dp"):
        other = yield swap(value, "dp", flip), 1
        value = jnp.concatenate([value, other], axis=dim)
    return value


def table_grad_of(requests, turn, embed_grad, padded_rows, all_rows):
    wanted = jnp.einsum("tr,td->rd", requests.chosen(turn), embed_grad, preferred_element_type=F32)
    wanted = wanted.astype(BF).reshape(lax.axis_size("vocab"), -1, embed_grad.shape[1])
    got = yield trade(split_blocks(wanted), "vocab"), 1
    got = yield from joined_dp(jnp.concatenate(got), 0)
    own = lax.axis_index("dp") * padded_rows + jnp.arange(padded_rows)[:, None]
    return jnp.dot((own == all_rows).astype(BF), got, preferred_element_type=F32)


def all_rounds(requests, start, one_round):
    def more(state):
        return state[0] < requests.rounds

    def again(state):
        return state[0] + 1, state[1] + one_round(state[0])

    return lax.while_loop(more, again, (jnp.int32(1), start))[1]


def moments(grad_part, first_part, second_part, master):
    new_first = beta_one * first_part + (1.0 - beta_one) * grad_part
    new_second = beta_two * second_part + (1.0 - beta_two) * grad_part * grad_part
    direction = (
        new_first
        / (1.0 - beta_one**step_count)
        / (jnp.sqrt(new_second / (1.0 - beta_two**step_count)) + adam_eps)
        + decay * master
    )
    return (new_first, new_second, direction)


def tensor_sums(arrays):
    attn, ffn, gains, table = arrays
    halfway = ffn.shape[2] // 2
    ffn_parts = jnp.stack(
        [
            jnp.sum(ffn[:, :, :halfway] ** 2, axis=(1, 2)),
            jnp.sum(ffn[:, :, halfway:] ** 2, axis=(1, 2)),
        ],
        axis=1,
    ).reshape(-1)
    return jnp.concatenate(
        [
            jnp.sum(attn * attn, axis=(1, 2)),
            ffn_parts,
            jnp.sum(gains * gains, axis=1),
            jnp.sum(table * table).reshape(1),
        ]
    )


def expand_ratios(ratio, halfway):
    ffn_ratio = jnp.repeat(ratio[12:16].reshape(2, 2), halfway, axis=1)[:, None, :]
    return (ratio[:12][:, None, None], ffn_ratio, ratio[16:23][:, None], ratio[23])


def side_by_side(matrices):
    return matrices.transpose(1, 0, 2).reshape(matrices.shape[1], -1)


def gather_rows(piece):
    return lax.all_gather(piece, ("dp", "vocab"), axis=0, tiled=True)


def gain_columns(gains):
    return jnp.pad(gains.T, ((0, 0), (0, LANES - gains.shape[0])))


def body(
    enc_ids,
    dec_ids,
    dec_mask,
    s_attn,
    s_ffn,
    s_gains,
    s_table,
    s_attn_m,
    s_attn_v,
    s_ffn_m,
    s_ffn_v,
    s_gains_m,
    s_gains_v,
    s_table_m,
    s_table_v,
    t_attn,
    t_ffn,
    t_gains,
    t_embed,
    t_head,
):
    vocab_count = lax.axis_size("vocab")
    dp_count = lax.axis_size("dp")
    vocab_index = lax.axis_index("vocab")
    seqs = enc_ids.shape[0]
    seq_dev = seqs // vocab_count
    enc_len = enc_ids.shape[1]
    dec_len = dec_ids.shape[1]
    total_seqs = seqs * dp_count
    width = s_attn.shape[2]
    t_width = t_attn.shape[2]
    ffn_width = s_ffn.shape[2]
    gain_count = s_gains.shape[0]
    out_scale = D_S ** (-0.5)

    low_attn, low_ffn = side_by_side(s_attn.astype(BF)), s_ffn.astype(BF)
    enc_pack = [low_attn[:, : 4 * width], low_ffn[0], gain_columns(s_gains.astype(BF))]
    dec_pack = [low_attn[:, 4 * width :], low_ffn[1]]
    bits = share_bits()
    core, first, middle, last = two_orders(bits)
    flows, table = Flows(), None
    order = middle + first + [last, core]
    flows.begin("enc", doubling(jnp.concatenate(enc_pack, axis=1), bits, order))
    order = middle + [last] + first + [core]
    flows.begin("dec", doubling(jnp.concatenate(dec_pack, axis=1), bits, order))

    part_rows = s_table.shape[0]
    padded_rows = -(-part_rows // LANES) * LANES
    padding = ((0, padded_rows - part_rows), (0, 0))
    dp_bits = [("dp", flip) for flip in flips("dp")]
    dp_order = list(range(len(dp_bits)))
    flows.begin("table", doubling(jnp.pad(s_table.astype(BF), padding), dp_bits, dp_order))
    part_columns = t_head.shape[1]
    head_part = t_head.reshape(dp_count, part_rows, part_columns)
    head_part = jnp.pad(head_part, ((0, 0),) + padding).reshape(-1, part_columns)
    in_use = jnp.arange(dp_count * padded_rows)[None, :] % padded_rows < part_rows
    ids = jnp.concatenate(
        [enc_ids.reshape(vocab_count, -1), dec_ids.reshape(vocab_count, -1)], axis=1
    )
    requests = Requests(relative(ids, "vocab"), part_rows, padded_rows)
    flows.begin("count", requests.counting())
    flows.begin("t_rows", teacher_rows_of(requests, jnp.int32(0), t_embed))
    teacher_parts = (
        jnp.concatenate([side_by_side(t_attn), t_ffn[0], gain_columns(t_gains)], axis=1),
        t_ffn[1],
    )
    for step in range(1, len(bits)):
        if step == GATHER_AFTER:
            teacher_parts = flows.turn(teacher_parts)
        else:
            flows.turn()
        if "table" in flows.results and "rows" not in flows.results and table is None:
            table = flows.results["table"].reshape(-1, width)
            flows.begin("rows", student_rows_of(requests, jnp.int32(0), table))
    teacher, teacher_last = [gather_rows(part) for part in teacher_parts]
    flows.finish()

    def student_round(turn):
        return run(student_rows_of(requests, turn, table))

    def teacher_round(turn):
        return run(teacher_rows_of(requests, turn, t_embed))

    embedded = all_rounds(requests, flows.results["rows"], student_round)
    t_embedded = all_rounds(requests, flows.results["t_rows"], teacher_round)
    enc_tokens = seq_dev * enc_len

    def parted(rows):
        return (
            rows[:enc_tokens].reshape(seq_dev, enc_len, -1),
            rows[enc_tokens:].reshape(seq_dev, dec_len, -1),
        )

    enc_in, dec_in = parted(embedded)
    t_enc_in, t_dec_in = parted(t_embedded)

    student_enc, student_dec = [
        flows.results[name].reshape(width, -1) for name in ("enc", "dec")
    ]
    flows.begin("head", pieces_by_xor(head_part, "dp"))
    flows.begin("asked", joined_dp(requests.listed(jnp.int32(0)).reshape(1, -1), 1))

    cut = 4 * width
    attn = [student_enc[:, :cut], student_dec[:, :cut], student_dec[:, cut : 2 * cut]]
    ffn = [student_enc[:, cut : cut + ffn_width], student_dec[:, 2 * cut :]]
    gains = student_enc[:, cut + ffn_width :].T[:gain_count]
    memory, enc_stored = encoder_forward(enc_in, attn[0], ffn[0], gains, relu_forward)
    memory = flows.turn(memory)
    head_in, dec_stored = decoder_forward(
        dec_in, memory, attn[1:], ffn[1], gains, relu_forward, out_scale
    )
    student_rows = spread(head_in.reshape(-1, width), "vocab")
    student_logit = [head_logits(rows, table, in_use) for rows in student_rows]
    student_sums = [logit_sums(logit) for logit in student_logit]

    thead = jnp.concatenate(flows.finish()["head"], axis=1)
    all_rows = flows.results["asked"]

    t_enc_in, student_sums = lax.optimization_barrier((t_enc_in, student_sums))
    cut = 4 * t_width
    tattn = [teacher[:, i * cut : (i + 1) * cut] for i in range(3)]
    tffn = teacher[:, 3 * cut : 3 * cut + t_ffn.shape[2]]
    tgains = teacher[:, 3 * cut + t_ffn.shape[2] :].T[:gain_count]
    t_memory, _ = encoder_forward(t_enc_in, tattn[0], tffn, tgains, gated_forward)
    t_head_in, _ = decoder_forward(
        t_dec_in, t_memory, tattn[1:], teacher_last, tgains, gated_forward, 1.0
    )
    t_head_rows = relative(t_head_in.reshape(-1, dp_count, part_columns), "dp", 1)
    t_head_rows = t_head_rows.reshape(-1, t_width)
    teacher_rows = spread(t_head_rows, "vocab")
    teacher_logit = [head_logits(rows, thead, in_use) for rows in teacher_rows]
    teacher_sums = [logit_sums(*logits) for logits in zip(teacher_logit, student_logit)]

    own_rows = seq_dev * dec_len
    sums = jnp.stack(
        [
            jnp.stack(student[:2] + teacher[:3])
            for student, teacher in zip(student_sums, teacher_sums)
        ],
        axis=1,
    )
    own_tops = sums[0], sums[2]
    for flip in flips("vocab")[::-1]:
        other = swap(sums, "vocab", flip)
        sums = merge_sums(sums, jnp.stack([other[:, i ^ flip] for i in range(vocab_count)], axis=1))
    student_lse = sums[0] + jnp.log(sums[1])
    teacher_lse = sums[2] + jnp.log(sums[3])
    kl_row = sums[4] / sums[3] - teacher_lse + student_lse
    end_mask = relative(dec_mask.astype(F32).reshape(vocab_count, seq_dev, dec_len), "vocab")
    row_weight = end_mask / (jnp.sum(end_mask, axis=2, keepdims=True) * total_seqs)
    row_weight = row_weight.reshape(vocab_count, own_rows)
    loss_sum = jnp.sum(row_weight[0] * kl_row[0])
    student_scale = row_weight * jnp.exp(own_tops[0] - student_lse)
    teacher_scale = row_weight * jnp.exp(own_tops[1] - teacher_lse)
    logit_grad = [
        (
            student_scale[k][:, None] * student_sums[k][-1].astype(F32)
            - teacher_scale[k][:, None] * teacher_sums[k][-1].astype(F32)
        ).astype(BF)
        for k in range(vocab_count)
    ]
    head_parts = [
        jnp.dot(grad, table, preferred_element_type=F32).astype(BF) for grad in logit_grad
    ]
    head_parts = trade(head_parts, "vocab")
    table_grad = lax.dot_general(
        jnp.concatenate(logit_grad),
        jnp.concatenate(student_rows),
        (((0,), (0,)), ((), ())),
        preferred_element_type=F32,
    ).astype(BF)
    head_parts, table_grad = lax.optimization_barrier((head_parts, table_grad))
    head_grad = sum(part.astype(F32) for part in head_parts).reshape(head_in.shape)
    flows = Flows()
    table_grad = table_grad.reshape((2,) * len(dp_bits) + (padded_rows, width))
    flows.begin("table", halving(table_grad, dp_bits, dp_order[::-1]))

    dec_in_grad, memory_grad, dec_gains = decoder_backward(
        flows, head_grad, dec_in, memory, dec_stored, attn[1:], ffn[1], gains, out_scale
    )
    enc_in_grad, enc_gains = encoder_backward(
        flows, memory_grad, enc_in, enc_stored, attn[0], ffn[0], gains
    )
    embed_grad = jnp.concatenate(
        [enc_in_grad.reshape(-1, width), dec_in_grad.reshape(-1, width)]
    ).astype(BF)

    flows.begin("rows", table_grad_of(requests, jnp.int32(0), embed_grad, padded_rows, all_rows))
    flows.begin("gains", adding(jnp.stack(enc_gains + dec_gains)))
    owned = flows.finish()

    def grad_round(turn):
        rows = run(joined_dp(requests.listed(turn).reshape(1, -1), 1))
        return run(table_grad_of(requests, turn, embed_grad, padded_rows, rows))

    table_grad = all_rounds(requests, owned["table"] + owned["rows"], grad_round)
    table_shard = table_grad[:part_rows]
    gain_sums = owned["gains"]
    share = lax.axis_index("dp") * vocab_count + vocab_index
    gains_shard = lax.dynamic_slice_in_dim(gain_sums, share * s_gains.shape[1], s_gains.shape[1], 1)

    def stacked(matrix):
        return matrix.reshape(matrix.shape[0], -1, width).transpose(1, 0, 2)

    attn_shard = jnp.concatenate(
        [stacked(owned[name]) for name in ("enc", "self", "cross")]
    )
    ffn_shard = jnp.stack([owned["enc_ffn"], owned["dec_ffn"]])

    gradients = (attn_shard, ffn_shard, gains_shard, table_shard)
    masters = (s_attn, s_ffn, s_gains, s_table)
    square_sum = sum((jnp.sum(part * part) for part in gradients))
    totals = jnp.concatenate([jnp.stack([square_sum, loss_sum]), tensor_sums(masters)])
    totals = sum_everywhere(totals)
    grad_norm = jnp.sqrt(totals[0])
    loss = totals[1]
    factor = jnp.minimum(1.0, clip_at / grad_norm)
    firsts = (s_attn_m, s_ffn_m, s_gains_m, s_table_m)
    seconds = (s_attn_v, s_ffn_v, s_gains_v, s_table_v)
    states = [
        moments(grad_part * factor, first_part, second_part, master)
        for grad_part, first_part, second_part, master in zip(gradients, firsts, seconds, masters)
    ]
    directions = tuple((state[2] for state in states))
    tensor_norm = jnp.sqrt(jnp.stack([totals[2:], sum_everywhere(tensor_sums(directions))]))
    ratio = tensor_norm[0] / (tensor_norm[1] + 1e-06)
    expanded = expand_ratios(ratio, s_ffn.shape[2] // 2)
    updates = [-rate * scale_part * state[2] for scale_part, state in zip(expanded, states)]
    return (
        states[0][0],
        states[0][1],
        updates[0],
        states[1][0],
        states[1][1],
        updates[1],
        states[2][0],
        states[2][1],
        updates[2],
        states[3][0],
        states[3][1],
        updates[3],
        tensor_norm,
        grad_norm,
        loss,
    )


def head_logits(rows, head, in_use):
    logit = lax.dot_general(rows, head, (((1,), (1,)), ((), ())), preferred_element_type=F32)
    return jnp.where(in_use, logit, masked_score)


def logit_sums(logit, other=None):
    top = jnp.max(logit, axis=1)
    weight = jnp.exp(logit - top[:, None])
    sums = [top, jnp.sum(weight, axis=1)]
    if other is not None:
        sums.append(jnp.sum(weight * (logit - other), axis=1))
    return sums + [lax.optimization_barrier(weight.astype(BF))]


def merge_sums(one, two):
    top = jnp.maximum(one[0], two[0])
    t_top = jnp.maximum(one[2], two[2])
    scale_one, scale_two = jnp.exp(one[2] - t_top), jnp.exp(two[2] - t_top)
    return jnp.stack(
        [
            top,
            one[1] * jnp.exp(one[0] - top) + two[1] * jnp.exp(two[0] - top),
            t_top,
            one[3] * scale_one + two[3] * scale_two,
            one[4] * scale_one + two[4] * scale_two,
        ]
    )


def solution(mesh):
    return jax.shard_map(
        body,
        mesh=mesh,
        in_specs=(
            P("dp", None),
            P("dp", None),
            P("dp", None),
            P(None, ("dp", "vocab"), None),
            P(None, ("dp", "vocab"), None),
            P(None, ("dp", "vocab")),
            P(("vocab", "dp"), None),
            P(None, ("dp", "vocab"), None),
            P(None, ("dp", "vocab"), None),
            P(None, ("dp", "vocab"), None),
            P(None, ("dp", "vocab"), None),
            P(None, ("dp", "vocab")),
            P(None, ("dp", "vocab")),
            P(("vocab", "dp"), None),
            P(("vocab", "dp"), None),
            P(None, ("dp", "vocab"), None),
            P(None, ("dp", "vocab"), None),
            P(None, ("dp", "vocab")),
            P("vocab", "dp"),
            P("vocab", "dp"),
        ),
        out_specs=(
            P(None, ("dp", "vocab"), None),
            P(None, ("dp", "vocab"), None),
            P(None, ("dp", "vocab"), None),
            P(None, ("dp", "vocab"), None),
            P(None, ("dp", "vocab"), None),
            P(None, ("dp", "vocab"), None),
            P(None, ("dp", "vocab")),
            P(None, ("dp", "vocab")),
            P(None, ("dp", "vocab")),
            P(("vocab", "dp"), None),
            P(("vocab", "dp"), None),
            P(("vocab", "dp"), None),
            P(),
            P(),
            P(),
        ),
        check_vma=False,
    )
```
